256 devices in a mesh: gy: 16 (over y, x), gx: 16 (over z, core).
Axes of the slice: x: 4, y: 4, z: 8, core: 2. Of those that a mesh axis runs over, the one named last changes fastest.
Arguments:
- direction: float32 [4, 64, 64, 1024], P(None, 'gx', 'gy'), may hold values from -6 to 6
- solution: float32 [4, 64, 64, 1024], P(None, 'gx', 'gy'), may hold values from -6 to 6
- residual: float32 [4, 64, 64, 1024], P(None, 'gx', 'gy'), may hold values from -6 to 6
- north_coef: float32 [64, 1024], P('gy'), may hold values from 0.12 to 0.25
- east_coef: float32 [64, 1024], P('gy'), may hold values from 0.12 to 0.25
- ocean: int32 [64, 1024], P('gy'), may hold values 0 or 1
- vert_coef: float32 [64, 64, 1024], P(None, 'gy', 'gx'), may hold values from 0.1 to 10
- obs_owner: int32 [16, 16, 512, 1], P('gy', 'gx'), may hold values from 0 to 255; in each aligned block of 512 rows (0 to 511, 512 to 1023, ..., all dimensions but the last counted through in order) at most 4 rows name the same one
- obs_row: int32 [16, 16, 512], P('gy', 'gx'), may hold values from 0 to 2
- obs_col: int32 [16, 16, 512], P('gy', 'gx'), may hold values from 0 to 62
- obs_frac: float32 [16, 16, 2, 512], P('gy', 'gx'), may hold values from 0 to 1
- error_inverse: float32 [16, 16, 256, 256], P('gy', 'gx'), may hold values from -3 to 6, as said below
Outputs:
- solution_next: float32 [4, 64, 64, 1024], P(None, 'gx', 'gy')
- residual_next: float32 [4, 64, 64, 1024], P(None, 'gx', 'gy')
- direction_next: float32 [4, 64, 64, 1024], P(None, 'gx', 'gy')
The draws below stay inside these ranges and needn't reach their ends.
Inputs may be any that keep to these rules, and one draw needn't show every extreme that they name: `obs_owner`: the observations of one device name each owner at most 4 times, and in every draw some device names some owner exactly 4 times. `error_inverse`: symmetric positive definite for every owner.
All inputs are finite; a program needn't handle non-finite values. No bound on the sum of `ocean` on one device may be relied on, other than what follows from the above.
Results may differ from the reference program's by a relative error of at most 0.000078.
Values sent between devices are 32-bit elements; how exact they have to be, the bound alone decides.
A program may use at most 128 MiB of HBM per device.

```python
import math
import jax
import jax.numpy as jnp
import numpy as np
from jax import lax

NVAR = 4
LAT_DEV = 4
LON_DEV = 64
NSTEP = 4
OBS_DEV = 512
NLEV = 64
NLAT = 64
NLON = 1024
KV = 256
CAP = 4
N_GY = 16
N_GX = 16


def draw_error_inverse(key, part):
    key_first, key_second = jax.random.split(jax.random.fold_in(key, 17))
    noise_draw = jnp.clip(jax.random.normal(key_first, (N_GY, N_GX, KV, KV), jnp.float32), -6.0, 6.0)
    symmetric = 0.5 * (noise_draw + jnp.swapaxes(noise_draw, 2, 3))
    scales = jnp.exp(jax.random.uniform(key_second, (N_GY, N_GX, 1, 1), jnp.float32, -0.6931472, 0.6931472))
    identity = jnp.eye(KV, dtype=jnp.float32)
    return scales * (1.6 * identity + 0.8 * symmetric / jnp.sqrt(jnp.float32(KV)))


def field_draw(key, salt):
    key_rough = jax.random.fold_in(jax.random.fold_in(key, salt), 0)
    field_shape = (NVAR, NLEV, NLAT, NLON)
    return jnp.clip(jax.random.normal(key_rough, field_shape, jnp.float32), -6.0, 6.0)


def draw_direction(key, part):
    return field_draw(key, 23)


def draw_residual(key, part):
    return field_draw(key, 29)


def with_ends(drawn, key, smallest, largest):
    extent = drawn.shape
    index_at = [jax.random.randint(jax.random.fold_in(key, axis), (), 0, extent[axis]) for axis in range(len(extent))]
    drawn = drawn.at[tuple(index_at)].set(smallest)
    longest = extent.index(max(extent))
    index_at[longest] = (index_at[longest] + 1) % extent[longest]
    return drawn.at[tuple(index_at)].set(largest)


def levels(key, shape, shards, low, high):
    gain, own = 1.0, jax.random.fold_in(key, 6)
    for axis_at, parts in shards:
        draws = jnp.exp(jax.random.uniform(jax.random.fold_in(own, axis_at), (parts,), jnp.float32, low / len(shards), high / len(shards)))
        gain = gain * jnp.repeat(draws, shape[axis_at] // parts).reshape([-1 if axis == axis_at else 1 for axis in range(len(shape))])
    return gain


def assign_block(own_key, own, number, rows, count, top, limit, lean):
    order = jax.random.permutation(own_key, count)
    packed, usual = load_shares(count, rows * top, limit, lean, True), load_shares(count, rows * top, limit, lean, False)
    places = jnp.arange(count)

    def named(tallies, turn):
        used = int((tallies > 0).sum())
        fixed = max(1, used // 4)
        shifted = fixed + (places - fixed + turn * (used - fixed)) % max(1, count - fixed)
        return jnp.zeros((count,), jnp.int32).at[order[jnp.where(places < fixed, places, shifted)]].set(jnp.asarray(tallies, jnp.int32))

    tallies = jnp.where(number % 4 == 0, named(packed, number // 4), named(usual, number - number // 4 - 1))
    mixed = jax.random.permutation(jax.random.fold_in(own, 3), count)
    donor, taker = mixed[0:count // 2 * 2:2], mixed[1:count // 2 * 2:2]
    room = jnp.minimum(tallies[donor] - 1, limit - tallies[taker]) // 2
    room = jnp.where((donor == order[0]) | (taker == order[0]) | (tallies[taker] == 0), 0, jnp.maximum(room, 0))
    shifted = jax.random.randint(jax.random.fold_in(own, 4), (count // 2,), 0, 1 << 20) % (room + 1)
    tallies = tallies.at[donor].add(-shifted).at[taker].add(shifted)
    items = jnp.searchsorted(jnp.cumsum(tallies), jnp.arange(rows * top), side="right").astype(jnp.int32)
    listing = items.reshape(top, rows).T
    listing = listing[jax.random.permutation(jax.random.fold_in(own, 1), rows)]
    turn = jax.random.randint(jax.random.fold_in(own, 2), (rows, 1), 0, top)
    return jnp.take_along_axis(listing, (jnp.arange(top)[None, :] + turn) % top, axis=1)


def load_shares(amount, total, bound, slope, full):
    weights = [(1 << 20) // math.isqrt(standing ** slope) + 1 for standing in range(1, amount + 1)]
    largest = bound if full else min(bound, max(-(-total // amount), total * weights[0] // sum(weights)))
    least = 1 if total - largest >= amount - 1 else 0
    holding, spare = [largest] + [least] * (amount - 1), total - largest - least * (amount - 1)
    while spare > 0:
        free = [i for i in range(1, amount) if holding[i] < largest] or [i for i in range(1, amount) if holding[i] < bound]
        whole, remaining = sum([weights[i] for i in free]), spare
        for i in free:
            addition = min(bound - holding[i], max(1, remaining * weights[i] // whole), spare)
            holding[i] = holding[i] + addition
            spare = spare - addition
    return np.array(holding)


def bell_draw(own_key, extent, scale, bound, shards=(), held_as=jnp.bfloat16):
    entries = jax.random.normal(own_key, extent, jnp.float32) * scale
    if len(shards) > 0:
        entries = levels(own_key, extent, shards, -0.22, 0.18) * entries
    return jnp.clip(entries, min=-bound, max=bound).astype(held_as)


def setup_inputs(seed: int = 0) -> dict:
    key_of = jax.random.split(jax.random.key(seed), 13)
    direction = draw_direction(jax.random.fold_in(key_of[12], 71), 0)
    solution = bell_draw(key_of[1], (NVAR, NLEV, NLAT, NLON), 1.0, 6.0, ((1, 16), (2, 16)), jnp.float32)
    residual = draw_residual(jax.random.fold_in(key_of[12], 71), 0)
    north_coef = jnp.clip(jnp.exp(math.log(0.25) - 0.7339692 * jax.random.uniform(key_of[3], (NLAT, NLON), jnp.float32) ** levels(key_of[3], (NLAT, NLON), ((0, 16),), -0.2, 0.2)), 0.12, 0.25)
    east_coef = jnp.clip(jnp.exp(math.log(0.25) - 0.7339692 * jax.random.uniform(key_of[4], (NLAT, NLON), jnp.float32) ** levels(key_of[4], (NLAT, NLON), ((0, 16),), -0.2, 0.2)), 0.12, 0.25)
    ocean = with_ends((jax.random.randint(key_of[5], (NLAT, NLON), 0, 10) < 9).astype(jnp.int32), jax.random.fold_in(key_of[5], 1), 0, 1)
    vert_coef = jnp.clip(jnp.exp(math.log(10.0) - 4.6051702 * jax.random.uniform(key_of[6], (NLEV, NLAT, NLON), jnp.float32) ** levels(key_of[6], (NLEV, NLAT, NLON), ((1, 16), (2, 16)), -0.2, 0.2)), 0.1, 10.0)
    obs_owner_keys = jax.random.split(jax.random.fold_in(key_of[7], 1), N_GY * N_GX * OBS_DEV // OBS_DEV)
    obs_owner_turns = jax.random.permutation(jax.random.fold_in(key_of[7], 3), N_GY * N_GX * OBS_DEV // OBS_DEV)
    obs_owner = jax.vmap(lambda own, number: assign_block(jax.random.fold_in(key_of[7], 2), own, number, OBS_DEV, N_GY * N_GX, 1, CAP, 2))(obs_owner_keys, obs_owner_turns).reshape((N_GY, N_GX, OBS_DEV, 1))
    obs_row = with_ends(jax.random.randint(key_of[8], (N_GY, N_GX, OBS_DEV), 0, LAT_DEV - 1), jax.random.fold_in(key_of[8], 1), 0, (LAT_DEV - 1) - 1).astype(jnp.int32)
    obs_col = with_ends(jax.random.randint(key_of[9], (N_GY, N_GX, OBS_DEV), 0, LON_DEV - 1), jax.random.fold_in(key_of[9], 1), 0, (LON_DEV - 1) - 1).astype(jnp.int32)
    obs_frac = jnp.clip(1.0 * jax.random.uniform(key_of[10], (N_GY, N_GX, 2, OBS_DEV), jnp.float32) ** levels(key_of[10], (N_GY, N_GX, 2, OBS_DEV), ((0, 16), (1, 16)), -0.2, 0.2), 0.0, 1.0)
    error_inverse = draw_error_inverse(jax.random.fold_in(key_of[12], 71), 0)
    return dict(direction=direction, solution=solution, residual=residual, north_coef=north_coef, east_coef=east_coef, ocean=ocean, vert_coef=vert_coef, obs_owner=obs_owner, obs_row=obs_row, obs_col=obs_col, obs_frac=obs_frac, error_inverse=error_inverse)


def lateral_faces(north_ext, east_ext, ocean_ext):
    ocean_next = jnp.concatenate([ocean_ext[1:], jnp.zeros_like(ocean_ext[:1])], axis=0)
    north_face = north_ext * ocean_ext * ocean_next
    east_face = east_ext * ocean_ext * jnp.roll(ocean_ext, -1, axis=1)
    return north_face, east_face, ocean_ext


def diffuse_once(values_grid, north_face, east_face, ocean_ext):
    north_flux = north_face[:-1] * (values_grid[:, :, 1:, :] - values_grid[:, :, :-1, :])
    east_flux = east_face * (jnp.roll(values_grid, -1, axis=3) - values_grid)
    lateral = east_flux - jnp.roll(east_flux, 1, axis=3)
    return (ocean_ext[1:-1] * values_grid[:, :, 1:-1, :] + north_flux[:, :, 1:, :] - north_flux[:, :, :-1, :]
            + lateral[:, :, 1:-1, :])


def lateral_whole(values_grid, faces):
    north_face, east_face, ocean_ext = faces
    for step_index in range(NSTEP):
        padded = jnp.pad(values_grid, ((0, 0), (0, 0), (1, 1), (0, 0)))
        values_grid = diffuse_once(padded, north_face, east_face, ocean_ext)
    return values_grid


def vertical_factors(vert_coef):
    inverse_rows = []
    upper_ratio = []
    for layer_index in range(vert_coef.shape[0]):
        diagonal = 1.0 + vert_coef[layer_index]
        if layer_index > 0:
            diagonal = diagonal + vert_coef[layer_index - 1] + vert_coef[layer_index - 1] * upper_ratio[-1]
        inverse = 1.0 / diagonal
        inverse_rows.append(inverse)
        upper_ratio.append(-vert_coef[layer_index] * inverse)
    return inverse_rows, upper_ratio


def vertical_solve(values_col, vert_coef, factors):
    inverse_rows, upper_ratio = factors
    layers = values_col.shape[1]
    forward = []
    for layer_index in range(layers):
        source = values_col[:, layer_index]
        if layer_index > 0:
            source = source + vert_coef[layer_index - 1] * forward[-1]
        forward.append(source * inverse_rows[layer_index])
    result = [forward[-1]]
    for layer_index in range(layers - 2, -1, -1):
        result.append(forward[layer_index] - upper_ratio[layer_index] * result[-1])
    return jnp.stack(result[::-1], axis=1)


def reference(direction, solution, residual, north_coef, east_coef, ocean, vert_coef, obs_owner, obs_row,
              obs_col, obs_frac, error_inverse):
    device_count = N_GY * N_GX
    pad_rows = ((1, 1), (0, 0))
    faces = lateral_faces(jnp.pad(north_coef, pad_rows), jnp.pad(east_coef, pad_rows),
                          jnp.pad(ocean.astype(jnp.float32), pad_rows))
    factors = vertical_factors(vert_coef)
    smoothed = vertical_solve(lateral_whole(direction, faces), vert_coef, factors)
    flat = smoothed.reshape(KV, NLAT * NLON)
    glob_row = jnp.arange(N_GY, dtype=jnp.int32)[:, None, None] * LAT_DEV + obs_row
    glob_col = jnp.arange(N_GX, dtype=jnp.int32)[None, :, None] * LON_DEV + obs_col
    cell = glob_row * NLON + glob_col
    corners = (cell, cell + 1, cell + NLON, cell + NLON + 1)
    lat_frac = obs_frac[:, :, 0, :]
    lon_frac = obs_frac[:, :, 1, :]
    weights = ((1.0 - lat_frac) * (1.0 - lon_frac), (1.0 - lat_frac) * lon_frac,
               lat_frac * (1.0 - lon_frac), lat_frac * lon_frac)
    profile = weights[0] * flat[:, corners[0]]
    for corner_index in range(1, 4):
        profile = profile + weights[corner_index] * flat[:, corners[corner_index]]
    owners = obs_owner[..., 0]
    onehot = (owners[..., None] == jnp.arange(device_count, dtype=jnp.int32)).astype(jnp.int32)
    running = jnp.cumsum(onehot, axis=2)
    rank_in = jnp.sum(running * onehot, axis=3) - 1
    source = (jnp.arange(N_GY, dtype=jnp.int32)[:, None, None] * N_GX
              + jnp.arange(N_GX, dtype=jnp.int32)[None, :, None]) + jnp.zeros_like(owners)
    slot = source * CAP + rank_in
    buffer = jnp.zeros((device_count, device_count * CAP, KV), jnp.float32)
    buffer = buffer.at[owners, slot].set(jnp.moveaxis(profile, 0, -1))
    weighted = jnp.einsum('osk,okl->osl', buffer, error_inverse.reshape(device_count, KV, KV),
                          precision=lax.Precision.HIGHEST)
    back = jnp.moveaxis(weighted[owners, slot], -1, 0)
    spread = jnp.zeros((KV, NLAT * NLON), jnp.float32)
    for corner_index in range(4):
        spread = spread.at[:, corners[corner_index]].add(weights[corner_index] * back)
    spread = spread.reshape(NVAR, NLEV, NLAT, NLON)
    image = direction + lateral_whole(vertical_solve(spread, vert_coef, factors), faces)
    norm_now = jnp.sum(residual * residual)
    alpha = norm_now / jnp.sum(direction * image)
    solution_next = solution + alpha * direction
    residual_next = residual - alpha * image
    norm_next = jnp.sum(residual_next * residual_next)
    direction_next = residual_next + (norm_next / norm_now) * direction
    return solution_next, residual_next, direction_next
```

```python
import functools

import jax
import jax.numpy as jnp
from jax import lax
from jax.experimental import pallas as pl
from jax.experimental.pallas import tpu as pltpu
from jax.sharding import PartitionSpec as P

NSTEP = 4
N = 16
F32 = jnp.float32
BF16 = jnp.bfloat16


def split(x):
    hi = x.astype(BF16)
    lo = (x - hi.astype(F32)).astype(BF16)
    return hi, lo


def dot(a, b, dims):
    return lax.dot_general(a, b, (dims, ((), ())), preferred_element_type=F32)


def dot3(a_hi, a_lo, b_hi, b_lo, dims):
    return dot(a_hi, b_hi, dims) + (dot(a_hi, b_lo, dims) + dot(a_lo, b_hi, dims))


def exchange(src, dst, axis, me, send_sem, recv_sem):
    def copy(peer, slot):
        return pltpu.make_async_remote_copy(
            src_ref=src(peer),
            dst_ref=dst(slot),
            send_sem=send_sem.at[peer],
            recv_sem=recv_sem.at[slot],
            device_id={axis: peer},
            device_id_type=pl.DeviceIdType.MESH,
        )

    def each(step):
        def body(d, carry):
            step(lax.rem(me + d, N))
            return carry

        lax.fori_loop(1, N, body, 0)

    def start():
        each(lambda peer: copy(peer, me).start())

    def wait_recv():
        each(lambda peer: copy(peer, peer).wait_recv())

    def wait_send():
        each(lambda peer: copy(peer, peer).wait_send())

    return start, wait_recv, wait_send


def kernel(
    dir_ref,
    res_ref,
    coef_ref,
    vert_ref,
    obs_ref,
    own_ref,
    err_ref,
    image_ref,
    scal_ref,
    ua,
    ub,
    uc,
    hc,
    cf,
    inv_ref,
    fa_ref,
    fb_ref,
    fw,
    c_hi,
    c_lo,
    w_hi,
    w_lo,
    e_hi,
    e_lo,
    xs1,
    xr1,
    sm,
    p_ref,
    r1,
    t2,
    a_ref,
    q_ref,
    b_ref,
    u_ref,
    back,
    sp,
    xs2,
    xr2,
    part,
    gat1,
    part2,
    gat2,
    hs_send,
    hs_recv,
    x_send,
    x_recv,
    o_send,
    o_recv,
    r_send,
    r_recv,
):
    gy = lax.axis_index("gy")
    gx = lax.axis_index("gx")

    barrier = pltpu.get_barrier_semaphore()

    def greet(d, carry):
        pl.semaphore_signal(
            barrier,
            inc=1,
            device_id={"gx": lax.rem(gx + d, N)},
            device_id_type=pl.DeviceIdType.MESH,
        )
        pl.semaphore_signal(
            barrier,
            inc=1,
            device_id={"gy": lax.rem(gy + d, N)},
            device_id_type=pl.DeviceIdType.MESH,
        )
        return carry

    lax.fori_loop(1, N, greet, 0)
    pl.semaphore_wait(barrier, 2 * (N - 1))

    def halo_copy(src, dst, sem, toward):
        return pltpu.make_async_remote_copy(
            src_ref=src,
            dst_ref=dst,
            send_sem=hs_send.at[sem],
            recv_sem=hs_recv.at[sem],
            device_id={"gy": toward},
            device_id_type=pl.DeviceIdType.MESH,
        )

    def halo(src, buf, sem):
        def up():
            return halo_copy(src, buf(0), sem, gy + 1)

        def down():
            return halo_copy(src, buf(2), sem + 1, gy - 1)

        def start():
            @pl.when(gy < N - 1)
            def _():
                up().start()

            @pl.when(gy > 0)
            def _():
                down().start()

        def wait_recv():
            @pl.when(gy > 0)
            def _():
                up().wait_recv()

            @pl.when(gy < N - 1)
            def _():
                down().wait_recv()

        def wait_send():
            @pl.when(gy < N - 1)
            def _():
                up().wait_send()

            @pl.when(gy > 0)
            def _():
                down().wait_send()

        return start, wait_recv, wait_send

    coef_halo = halo(coef_ref, lambda b: hc.at[b], 0)
    first_halo = [
        halo(dir_ref.at[h], lambda b, h=h: ua.at[h, pl.ds(4 * b, 4)], 2 + 2 * h)
        for h in range(2)
    ]
    second_halo = [
        halo(uc.at[h, pl.ds(4, 4)], lambda b, h=h: uc.at[h, pl.ds(4 * b, 4)], 6 + 2 * h)
        for h in range(2)
    ]
    coef_halo[0]()
    first_halo[0][0]()
    first_halo[1][0]()

    @pl.when(gy == 0)
    def _():
        hc[0] = jnp.zeros((3, 4, 1024), F32)
        for h in range(2):
            ua[h, pl.ds(0, 4)] = jnp.zeros((4, 8, 1024), F32)
            uc[h, pl.ds(0, 4)] = jnp.zeros((4, 8, 1024), F32)

    @pl.when(gy == N - 1)
    def _():
        hc[2] = jnp.zeros((3, 4, 1024), F32)
        for h in range(2):
            ua[h, pl.ds(8, 4)] = jnp.zeros((4, 8, 1024), F32)
            uc[h, pl.ds(8, 4)] = jnp.zeros((4, 8, 1024), F32)

    hc[1] = coef_ref[...]
    ua[:, pl.ds(4, 4)] = dir_ref[...]

    def factor_row(i, carry):
        v_prev, up_prev = carry
        v = vert_ref[i]
        diagonal = 1.0 + v + v_prev + v_prev * up_prev
        inverse = 1.0 / diagonal
        ratio = v * inverse
        inv_ref[i] = inverse
        fa_ref[i] = v_prev * inverse
        fb_ref[i] = ratio
        return v, -ratio

    zero_row = jnp.zeros((4, 128), F32)
    lax.fori_loop(0, 64, factor_row, (zero_row, zero_row))

    owner_row = own_ref[0:1, :]
    lane512 = lax.broadcasted_iota(jnp.int32, (64, 512), 1)
    sub512 = lax.broadcasted_iota(jnp.int32, (64, 512), 0)
    cell = lax.broadcasted_iota(jnp.int32, (64, 256), 1)
    cell_row = (cell // 64).astype(F32)
    cell_lon = (cell % 64).astype(F32)

    def obs_group(g, rank):
        rows = pl.ds(pl.multiple_of(64 * g, 64), 64)
        block = obs_ref[rows, :]
        o, r, c = block[:, 0:1], block[:, 1:2], block[:, 2:3]
        fr, fc = block[:, 3:4], block[:, 4:5]
        lat = jnp.where(cell_row == r, 1.0 - fr, jnp.where(cell_row == r + 1.0, fr, 0.0))
        lon = jnp.where(cell_lon == c, 1.0 - fc, jnp.where(cell_lon == c + 1.0, fc, 0.0))
        hi, lo = split(lat * lon)
        c_hi[rows, :] = hi
        c_lo[rows, :] = lo
        same = (o == owner_row) & (sub512 + 64 * g < lane512)
        return rank + jnp.sum(jnp.where(same, 1.0, 0.0), axis=0, keepdims=True)

    rank = lax.fori_loop(0, 8, obs_group, jnp.zeros((1, 512), F32))
    owner_int = owner_row.astype(jnp.int32)
    slot = ((owner_int % N) * N + owner_int // N) * 4 + rank.astype(jnp.int32)

    def slot_group(g, carry):
        base = pl.multiple_of(256 * g, 256)
        sub = lax.broadcasted_iota(jnp.int32, (256, 512), 0) + base
        hot = jnp.where(sub == slot, 1.0, 0.0).astype(BF16)
        rows = pl.ds(base, 256)
        w_hi[rows, :] = dot(hot, c_hi[...], ((1,), (0,))).astype(BF16)
        w_lo[rows, :] = dot(hot, c_lo[...], ((1,), (0,))).astype(BF16)
        return carry

    lax.fori_loop(0, 4, slot_group, 0)
    hi, lo = split(err_ref[...])
    e_hi[...] = hi
    e_lo[...] = lo

    def zero_tile():
        return jnp.zeros((8, 1024), F32)

    def rr_group(i, acc):
        x = res_ref[i // 4, i % 4]
        return acc + x * x

    rr = lax.fori_loop(0, 8, rr_group, zero_tile())

    coef_halo[1]()

    def coef_row(i, q):
        return hc[i // 4, q, i % 4 : i % 4 + 1, :]

    fn_prev = jnp.zeros((1, 1024), F32)
    for i in range(12):
        m = coef_row(i, 2)
        if i < 11:
            fn = coef_row(i, 0) * m * coef_row(i + 1, 2)
        else:
            fn = jnp.zeros((1, 1024), F32)
        fe = coef_row(i, 1) * m * pltpu.roll(m, 1023, 1)
        fw_e = pltpu.roll(fe, 1, 1)
        centre = m - fn - fn_prev - fe - fw_e
        for q, value in enumerate((centre, fn, fe, fw_e)):
            cf[i, q] = jnp.broadcast_to(value, (8, 1024))
        fn_prev = fn

    def stencil(src, h, i):
        u = src[h, i]
        return (
            cf[i, 0] * u
            + cf[i, 1] * src[h, i + 1]
            + cf[i - 1, 1] * src[h, i - 1]
            + cf[i, 2] * pltpu.roll(u, 1023, 1)
            + cf[i, 3] * pltpu.roll(u, 1, 1)
        )

    def lateral(buf, h):
        src, dst = buf, ub
        for step in range(NSTEP - 1):

            def row(i, carry, src=src, dst=dst):
                dst[h, i] = stencil(src, h, i)
                return carry

            lax.fori_loop(1 + step, 11 - step, row, 0)
            src, dst = dst, src
        return src

    low = lax.broadcasted_iota(jnp.int32, (8, 128), 1) < 64

    def swap(a, b):
        return (
            jnp.where(low, a, pltpu.roll(b, 64, 1)),
            jnp.where(low, pltpu.roll(a, 64, 1), b),
        )

    x1 = [
        exchange(
            lambda p, h=h: xs1.at[h, p],
            lambda s, h=h: xr1.at[h, s],
            "gx",
            gx,
            x_send.at[h],
            x_recv.at[h],
        )
        for h in range(2)
    ]
    x2 = [
        exchange(
            lambda p, h=h: xs2.at[h, p],
            lambda s, h=h: xr2.at[h, s],
            "gx",
            gx,
            x_send.at[2 + h],
            x_recv.at[2 + h],
        )
        for h in range(2)
    ]

    for h in range(2):
        first_halo[h][1]()
        src = lateral(ua, h)
        for pair in range(2):
            a = stencil(src, h, 4 + 2 * pair)
            b = stencil(src, h, 5 + 2 * pair)
            for t in range(8):
                lanes = slice(128 * t, 128 * t + 128)
                even, odd = swap(a[:, lanes], b[:, lanes])
                xs1[h, 2 * t, 8 * pair : 8 * pair + 8] = even
                xs1[h, 2 * t + 1, 8 * pair : 8 * pair + 8] = odd
        x1[h][0]()
        xr1[h, gx] = xs1[h, gx]

    def vertical(load, store):
        def forward(j, prev):
            for i in range(8):
                k = 8 * j + i
                prev = load(j, i) * inv_ref[k] + fa_ref[k] * prev
                fw[k] = prev
            return prev

        lax.fori_loop(0, 8, forward, zero_row)

        def backward(k, prev):
            j = 7 - k
            for i in range(7, -1, -1):
                prev = fw[8 * j + i] + fb_ref[8 * j + i] * prev
                store(j, i, prev)
            return prev

        lax.fori_loop(0, 8, backward, zero_row)

    def obs_exchange(src, dst, axis, me, k):
        return [
            exchange(
                lambda p, h=h: src(h, p),
                lambda s, h=h: dst(h, s),
                axis,
                me,
                o_send.at[2 * k + h],
                o_recv.at[2 * k + h],
            )
            for h in range(2)
        ]

    o1 = obs_exchange(lambda h, p: p_ref.at[h, p], lambda h, s: r1.at[h, s], "gx", gx, 0)
    o2 = obs_exchange(lambda h, p: t2.at[h, p // 2, p % 2], lambda h, s: a_ref.at[h, s], "gy", gy, 1)
    o3 = obs_exchange(lambda h, p: q_ref.at[h, p], lambda h, s: b_ref.at[h, s], "gy", gy, 2)
    o4 = obs_exchange(lambda h, p: u_ref.at[h, p // 2, p % 2], lambda h, s: back.at[h, s], "gx", gx, 3)

    for h in range(2):
        x1[h][1]()

        def load_column(j, i, h=h):
            return xr1[h, 2 * j + i // 4, pl.ds(i % 4, 4, stride=4), :]

        def store_column(j, i, value, h=h):
            sm[h, pl.ds(8 * j + i, 4, stride=64), :] = value

        vertical(load_column, store_column)
        s_hi, s_lo = split(jnp.concatenate([sm[h, 0:128], sm[h, 128:256]], axis=1))

        def profile(c, carry, h=h, s_hi=s_hi, s_lo=s_lo):
            rows = pl.ds(pl.multiple_of(256 * c, 256), 256)
            value = dot3(w_hi[rows, :], w_lo[rows, :], s_hi, s_lo, ((1,), (1,)))
            p_ref[h, pl.ds(4 * c, 4)] = value.reshape(4, 8, 8, 128)
            return carry

        lax.fori_loop(0, 4, profile, 0)
        o1[h][0]()
        r1[h, gx] = p_ref[h, gx]

    top = lax.broadcasted_iota(jnp.int32, (8, 8, 128), 1) < 4

    def interleave(src, dst, h):
        def pair(p, carry):
            a, b = src[h, 2 * p], src[h, 2 * p + 1]
            dst[h, :, 0, p] = jnp.where(top, a, pltpu.roll(b, 4, 1))
            dst[h, :, 1, p] = jnp.where(top, pltpu.roll(a, 4, 1), b)
            return carry

        lax.fori_loop(0, 8, pair, 0)

    for h in range(2):
        o1[h][1]()
        interleave(r1, t2, h)
        o2[h][0]()
        a_ref[h, gy] = t2[h, gy // 2, gy % 2]
    o2[0][1]()
    o2[1][1]()

    def weigh(c, carry):
        blocks = [a_ref[h, pl.ds(4 * c, 4)].reshape(256, 128) for h in range(2)]
        hi, lo = split(jnp.concatenate(blocks, axis=1))
        value = dot3(hi, lo, e_hi[...], e_lo[...], ((1,), (0,)))
        for h in range(2):
            q_ref[h, pl.ds(4 * c, 4)] = value[:, 128 * h : 128 * h + 128].reshape(4, 8, 8, 128)
        return carry

    lax.fori_loop(0, 4, weigh, 0)
    for h in range(2):
        o3[h][0]()
        b_ref[h, gy] = q_ref[h, gy]
    for h in range(2):
        o3[h][1]()
        interleave(b_ref, u_ref, h)
        o4[h][0]()
        back[h, gx] = u_ref[h, gx // 2, gx % 2]

    for h in range(2):
        o4[h][1]()
        b_hi, b_lo = split(back[h].reshape(1024, 128))
        spread = dot3(b_hi, b_lo, w_hi[...], w_lo[...], ((0,), (0,)))
        sp[h, 0:128] = spread[:, 0:128]
        sp[h, 128:256] = spread[:, 128:256]

        def load_spread(j, i, h=h):
            return sp[h, pl.ds(8 * j + i, 4, stride=64), :]

        def store_spread(j, i, value, h=h):
            xs2[h, 2 * j + i // 4, pl.ds(i % 4, 4, stride=4), :] = value

        vertical(load_spread, store_spread)
        x2[h][0]()
        xr2[h, gx] = xs2[h, gx]

    for h in range(2):
        x2[h][1]()
        for pair in range(2):
            rows = slice(8 * pair, 8 * pair + 8)
            for t in range(8):
                a, b = swap(xr2[h, 2 * t, rows], xr2[h, 2 * t + 1, rows])
                uc[h, 4 + 2 * pair, :, 128 * t : 128 * t + 128] = a
                uc[h, 5 + 2 * pair, :, 128 * t : 128 * t + 128] = b
        second_halo[h][0]()

    sums = (zero_tile(), zero_tile(), zero_tile())
    for h in range(2):
        second_halo[h][1]()
        second_halo[h][2]()
        src = lateral(uc, h)

        def last(i, carry, h=h, src=src):
            pq, rq, qq = carry
            d, r = dir_ref[h, i], res_ref[h, i]
            q = d + stencil(src, h, i + 4)
            image_ref[h, i] = q
            return pq + d * q, rq + r * q, qq + q * q

        sums = lax.fori_loop(0, 4, last, sums)

    def fold(x):
        total = x[:, 0:128]
        for t in range(1, 8):
            total = total + x[:, 128 * t : 128 * t + 128]
        return jnp.sum(total, axis=0, keepdims=True)

    rows = [fold(x) for x in (rr, *sums)]
    part[...] = jnp.concatenate(rows + [jnp.zeros((4, 128), F32)], axis=0)
    g1 = exchange(lambda p: part, lambda s: gat1.at[s], "gx", gx, r_send.at[0], r_recv.at[0])
    g2 = exchange(lambda p: part2, lambda s: gat2.at[s], "gy", gy, r_send.at[1], r_recv.at[1])
    g1[0]()
    gat1[gx] = part[...]
    g1[1]()
    part2[...] = jnp.sum(gat1[...], axis=0)
    g2[0]()
    gat2[gy] = part2[...]
    g2[1]()
    total = jnp.sum(jnp.sum(gat2[...], axis=0), axis=1, keepdims=True)
    norm_now, curvature = total[0:1], total[1:2]
    cross, image_norm = total[2:3], total[3:4]
    alpha = norm_now / curvature
    norm_next = norm_now - 2.0 * alpha * cross + alpha * alpha * image_norm
    beta = norm_next / norm_now
    scal_ref[...] = jnp.concatenate(
        [jnp.broadcast_to(alpha, (4, 128)), jnp.broadcast_to(beta, (4, 128))], axis=0
    )

    coef_halo[2]()
    for h in range(2):
        first_halo[h][2]()
        for group in (x1, x2, o1, o2, o3, o4):
            group[h][2]()
    g1[2]()
    g2[2]()


def per_device(
    direction,
    solution,
    residual,
    north_coef,
    east_coef,
    ocean,
    vert_coef,
    obs_owner,
    obs_row,
    obs_col,
    obs_frac,
    error_inverse,
):
    def by_row(x):
        return x.reshape(2, 2, 4, 4, 1024).transpose(0, 3, 1, 2, 4).reshape(2, 4, 8, 1024)

    coef = jnp.stack([north_coef, east_coef, ocean.astype(F32)])
    owner = obs_owner.reshape(512).astype(F32)
    obs = jnp.stack(
        [
            owner,
            obs_row.reshape(512).astype(F32),
            obs_col.reshape(512).astype(F32),
            obs_frac[0, 0, 0],
            obs_frac[0, 0, 1],
        ],
        axis=1,
    )
    vm = pltpu.VMEM
    dma = pltpu.SemaphoreType.DMA
    obs_buf = vm((2, N, 8, 8, 128), F32)
    mix_buf = vm((2, 8, 2, 8, 8, 128), F32)
    image, scal = pl.pallas_call(
        kernel,
        out_shape=(
            jax.ShapeDtypeStruct((2, 4, 8, 1024), F32),
            jax.ShapeDtypeStruct((8, 128), F32),
        ),
        in_specs=[pl.BlockSpec(memory_space=pltpu.VMEM)] * 7,
        out_specs=(pl.BlockSpec(memory_space=pltpu.VMEM),) * 2,
        scratch_shapes=[
            vm((2, 12, 8, 1024), F32),
            vm((2, 12, 8, 1024), F32),
            vm((2, 12, 8, 1024), F32),
            vm((3, 3, 4, 1024), F32),
            vm((12, 4, 8, 1024), F32),
            vm((64, 4, 128), F32),
            vm((64, 4, 128), F32),
            vm((64, 4, 128), F32),
            vm((64, 4, 128), F32),
            vm((512, 256), BF16),
            vm((512, 256), BF16),
            vm((1024, 256), BF16),
            vm((1024, 256), BF16),
            vm((256, 256), BF16),
            vm((256, 256), BF16),
            vm((2, N, 16, 128), F32),
            vm((2, N, 16, 128), F32),
            vm((2, 256, 128), F32),
            obs_buf,
            obs_buf,
            mix_buf,
            obs_buf,
            obs_buf,
            obs_buf,
            mix_buf,
            obs_buf,
            vm((2, 256, 128), F32),
            vm((2, N, 16, 128), F32),
            vm((2, N, 16, 128), F32),
            vm((8, 128), F32),
            vm((N, 8, 128), F32),
            vm((8, 128), F32),
            vm((N, 8, 128), F32),
            dma((10,)),
            dma((10,)),
            dma((4, N)),
            dma((4, N)),
            dma((8, N)),
            dma((8, N)),
            dma((2, N)),
            dma((2, N)),
        ],
        compiler_params=pltpu.CompilerParams(collective_id=0, has_side_effects=True),
        name="cg_step",
    )(
        by_row(direction),
        by_row(residual),
        coef,
        jnp.repeat(vert_coef.reshape(64, 2, 128), 2, axis=1),
        obs,
        owner.reshape(1, 512),
        error_inverse.reshape(256, 256),
    )
    image = image.reshape(2, 4, 2, 4, 1024).transpose(0, 2, 3, 1, 4).reshape(4, 4, 4, 1024)
    alpha = scal[0, 0]
    beta = scal[4, 0]
    residual_next = residual - alpha * image
    solution_next = solution + alpha * direction
    direction_next = residual_next + beta * direction
    return (solution_next, residual_next, direction_next)


def solution(mesh):
    field = P(None, "gx", "gy", None)
    in_specs = (
        field,
        field,
        field,
        P("gy", None),
        P("gy", None),
        P("gy", None),
        P(None, "gy", "gx"),
        P("gy", "gx", None, None),
        P("gy", "gx", None),
        P("gy", "gx", None),
        P("gy", "gx", None, None),
        P("gy", "gx", None, None),
    )
    return jax.shard_map(
        per_device, mesh=mesh, in_specs=in_specs, out_specs=(field,) * 3, check_vma=False
    )
```

```python
import functools

import jax
import jax.numpy as jnp
from jax import lax
from jax.experimental import pallas as pl
from jax.experimental.pallas import tpu as pltpu
from jax.sharding import PartitionSpec as P

NSTEP = 4
N = 16
F32 = jnp.float32
BF16 = jnp.bfloat16


def split(x):
    hi = x.astype(BF16)
    lo = (x - hi.astype(F32)).astype(BF16)
    return hi, lo


def dot(a, b, dims):
    return lax.dot_general(a, b, (dims, ((), ())), preferred_element_type=F32)


def dot3(a_hi, a_lo, b_hi, b_lo, dims):
    return dot(a_hi, b_hi, dims) + (dot(a_hi, b_lo, dims) + dot(a_lo, b_hi, dims))


def exchange(src, dst, axis, me, send_sem, recv_sem):
    def copy(peer, slot):
        return pltpu.make_async_remote_copy(
            src_ref=src(peer),
            dst_ref=dst(slot),
            send_sem=send_sem.at[peer],
            recv_sem=recv_sem.at[slot],
            device_id={axis: peer},
            device_id_type=pl.DeviceIdType.MESH,
        )

    def each(step):
        def body(d, carry):
            step(lax.rem(me + d, N))
            return carry

        lax.fori_loop(1, N, body, 0)

    def start():
        each(lambda peer: copy(peer, me).start())

    def wait_recv():
        each(lambda peer: copy(peer, peer).wait_recv())

    def wait_send():
        each(lambda peer: copy(peer, peer).wait_send())

    return start, wait_recv, wait_send


OFFSETS = ((3, -3), (0, 4), (2, -2), (1, -1))


def kernel(
    dir_ref,
    res_ref,
    north_ref,
    east_ref,
    ocean_ref,
    vert_ref,
    own_ref,
    row_ref,
    col_ref,
    frac_ref,
    err_ref,
    image_ref,
    scal_ref,
    dt,
    ua,
    ub,
    uc,
    hn,
    he,
    ho,
    cf,
    obs_ref,
    vb,
    inv_ref,
    fa_ref,
    fb_ref,
    fw,
    c_hi,
    c_lo,
    w_hi,
    w_lo,
    e_hi,
    e_lo,
    xs1,
    xr1,
    sm,
    p_ref,
    r1,
    t2,
    a_ref,
    q_ref,
    b_ref,
    u_ref,
    back,
    sp,
    xs2,
    xr2,
    part,
    gat1,
    part2,
    gat2,
    hs_send,
    hs_recv,
    x_send,
    x_recv,
    o1_send,
    o1_recv,
    o2_send,
    o2_recv,
    o3_send,
    o3_recv,
    o4_send,
    o4_recv,
    r_send,
    r_recv,
):
    gy = lax.axis_index("gy")
    gx = lax.axis_index("gx")

    barrier = pltpu.get_barrier_semaphore()

    def greet(d, carry):
        pl.semaphore_signal(
            barrier,
            inc=1,
            device_id={"gx": lax.rem(gx + d, N)},
            device_id_type=pl.DeviceIdType.MESH,
        )
        pl.semaphore_signal(
            barrier,
            inc=1,
            device_id={"gy": lax.rem(gy + d, N)},
            device_id_type=pl.DeviceIdType.MESH,
        )
        return carry

    lax.fori_loop(1, N, greet, 0)

    for h in range(2):
        for r in range(4):
            rows = [dir_ref[2 * h + v, l, r : r + 1, :] for v in range(2) for l in range(4)]
            tile = jnp.concatenate(rows, axis=0)
            dt[h, r] = tile
            ua[h, 4 + r] = tile

    owner_row = own_ref[...].astype(F32)
    table = jnp.concatenate(
        [
            owner_row,
            row_ref[...].astype(F32),
            col_ref[...].astype(F32),
            frac_ref[...],
            jnp.zeros((123, 512), F32),
        ],
        axis=0,
    )
    for g in range(4):
        obs_ref[128 * g : 128 * g + 128, :] = table[:, 128 * g : 128 * g + 128].T
    lane512 = lax.broadcasted_iota(jnp.int32, (64, 512), 1)
    sub512 = lax.broadcasted_iota(jnp.int32, (64, 512), 0)
    cell = lax.broadcasted_iota(jnp.int32, (64, 256), 1)
    cell_row = (cell // 64).astype(F32)
    cell_lon = (cell % 64).astype(F32)

    def obs_group(g, rank):
        rows = pl.ds(pl.multiple_of(64 * g, 64), 64)
        block = obs_ref[rows, :]
        o, r, c = block[:, 0:1], block[:, 1:2], block[:, 2:3]
        fr, fc = block[:, 3:4], block[:, 4:5]
        lat = jnp.where(cell_row == r, 1.0 - fr, jnp.where(cell_row == r + 1.0, fr, 0.0))
        lon = jnp.where(cell_lon == c, 1.0 - fc, jnp.where(cell_lon == c + 1.0, fc, 0.0))
        hi, lo = split(lat * lon)
        c_hi[rows, :] = hi
        c_lo[rows, :] = lo
        same = (o == owner_row) & (sub512 + 64 * g < lane512)
        return rank + jnp.sum(jnp.where(same, 1.0, 0.0), axis=0, keepdims=True)

    rank = lax.fori_loop(0, 8, obs_group, jnp.zeros((1, 512), F32))
    owner_int = own_ref[...]
    slot = ((owner_int % N) * N + owner_int // N) * 4 + rank.astype(jnp.int32)

    def slot_group(g, carry):
        base = pl.multiple_of(256 * g, 256)
        sub = lax.broadcasted_iota(jnp.int32, (256, 512), 0) + base
        hot = jnp.where(sub == slot, 1.0, 0.0).astype(BF16)
        rows = pl.ds(base, 256)
        w_hi[rows, :] = dot(hot, c_hi[...], ((1,), (0,))).astype(BF16)
        w_lo[rows, :] = dot(hot, c_lo[...], ((1,), (0,))).astype(BF16)
        return carry

    lax.fori_loop(0, 4, slot_group, 0)
    hi, lo = split(err_ref[...])
    e_hi[...] = hi
    e_lo[...] = lo

    pl.semaphore_wait(barrier, 2 * (N - 1))

    def halo_copy(src, dst, sem, toward):
        return pltpu.make_async_remote_copy(
            src_ref=src,
            dst_ref=dst,
            send_sem=hs_send.at[sem],
            recv_sem=hs_recv.at[sem],
            device_id={"gy": toward},
            device_id_type=pl.DeviceIdType.MESH,
        )

    def halo(src, buf, sem):
        def up():
            return halo_copy(src, buf(0), sem, gy + 1)

        def down():
            return halo_copy(src, buf(2), sem + 1, gy - 1)

        def start():
            @pl.when(gy < N - 1)
            def _():
                up().start()

            @pl.when(gy > 0)
            def _():
                down().start()

        def wait_recv():
            @pl.when(gy > 0)
            def _():
                up().wait_recv()

            @pl.when(gy < N - 1)
            def _():
                down().wait_recv()

        def wait_send():
            @pl.when(gy < N - 1)
            def _():
                up().wait_send()

            @pl.when(gy > 0)
            def _():
                down().wait_send()

        return start, wait_recv, wait_send

    coef_halos = [
        halo(north_ref, lambda b: hn.at[b], 0),
        halo(east_ref, lambda b: he.at[b], 2),
        halo(ocean_ref, lambda b: ho.at[b], 4),
    ]
    first_halo = [
        halo(dt.at[h], lambda b, h=h: ua.at[h, pl.ds(4 * b, 4)], 6 + 2 * h) for h in range(2)
    ]
    second_halo = [
        halo(uc.at[h, pl.ds(4, 4)], lambda b, h=h: uc.at[h, pl.ds(4 * b, 4)], 10 + 2 * h)
        for h in range(2)
    ]
    for group in coef_halos:
        group[0]()
    first_halo[0][0]()
    first_halo[1][0]()

    @pl.when(gy == 0)
    def _():
        hn[0] = jnp.zeros((4, 1024), F32)
        he[0] = jnp.zeros((4, 1024), F32)
        ho[0] = jnp.zeros((4, 1024), jnp.int32)
        for h in range(2):
            ua[h, pl.ds(0, 4)] = jnp.zeros((4, 8, 1024), F32)
            uc[h, pl.ds(0, 4)] = jnp.zeros((4, 8, 1024), F32)

    @pl.when(gy == N - 1)
    def _():
        hn[2] = jnp.zeros((4, 1024), F32)
        he[2] = jnp.zeros((4, 1024), F32)
        ho[2] = jnp.zeros((4, 1024), jnp.int32)
        for h in range(2):
            ua[h, pl.ds(8, 4)] = jnp.zeros((4, 8, 1024), F32)
            uc[h, pl.ds(8, 4)] = jnp.zeros((4, 8, 1024), F32)

    hn[1] = north_ref[...]
    he[1] = east_ref[...]
    ho[1] = ocean_ref[...]

    def spread_row(i, carry):
        v = vert_ref[i]
        left = jnp.concatenate([v[0:1], v[0:1], v[2:3], v[2:3]], axis=0)
        right = jnp.concatenate([v[1:2], v[1:2], v[3:4], v[3:4]], axis=0)
        vb[i] = jnp.concatenate([left, right], axis=1)
        return carry

    lax.fori_loop(0, 64, spread_row, 0)

    def factor_row(i, carry):
        v_prev, up_prev = carry
        v = vb[i]
        diagonal = 1.0 + v + v_prev + v_prev * up_prev
        inverse = 1.0 / diagonal
        ratio = v * inverse
        inv_ref[i] = inverse
        fa_ref[i] = v_prev * inverse
        fb_ref[i] = ratio
        return v, -ratio

    zero_row = jnp.zeros((4, 128), F32)
    lax.fori_loop(0, 64, factor_row, (zero_row, zero_row))

    def zero_tile():
        return jnp.zeros((4, 1024), F32)

    def rr_group(i, acc):
        x = res_ref[i // 4, i % 4]
        return acc + x * x

    rr = lax.fori_loop(0, 16, rr_group, zero_tile())

    for group in coef_halos:
        group[1]()

    def coef_row(i, q):
        buf = (hn, he, ho)[q]
        return buf[i // 4, i % 4 : i % 4 + 1, :].astype(F32)

    fn_prev = jnp.zeros((1, 1024), F32)
    for i in range(12):
        m = coef_row(i, 2)
        if i < 11:
            fn = coef_row(i, 0) * m * coef_row(i + 1, 2)
        else:
            fn = jnp.zeros((1, 1024), F32)
        fe = coef_row(i, 1) * m * pltpu.roll(m, 1023, 1)
        fw_e = pltpu.roll(fe, 1, 1)
        centre = m - fn - fn_prev - fe - fw_e
        for q, value in enumerate((centre, fn, fe, fw_e)):
            cf[i, q] = jnp.broadcast_to(value, (8, 1024))
        fn_prev = fn

    def stencil(src, h, i):
        u = src[h, i]
        return (
            cf[i, 0] * u
            + cf[i, 1] * src[h, i + 1]
            + cf[i - 1, 1] * src[h, i - 1]
            + cf[i, 2] * pltpu.roll(u, 1023, 1)
            + cf[i, 3] * pltpu.roll(u, 1, 1)
        )

    def lateral(buf, h):
        src, dst = buf, ub
        for step in range(NSTEP - 1):

            def row(i, carry, src=src, dst=dst):
                dst[h, i] = stencil(src, h, i)
                return carry

            lax.fori_loop(1 + step, 11 - step, row, 0)
            src, dst = dst, src
        return src

    low = lax.broadcasted_iota(jnp.int32, (8, 128), 1) < 64

    def swap(a, b):
        return (
            jnp.where(low, a, pltpu.roll(b, 64, 1)),
            jnp.where(low, pltpu.roll(a, 64, 1), b),
        )

    x1 = [
        exchange(
            lambda p, h=h: xs1.at[h, p],
            lambda s, h=h: xr1.at[h, s],
            "gx",
            gx,
            x_send.at[h],
            x_recv.at[h],
        )
        for h in range(2)
    ]
    x2 = [
        exchange(
            lambda p, h=h: xs2.at[h, p],
            lambda s, h=h: xr2.at[h, s],
            "gx",
            gx,
            x_send.at[2 + h],
            x_recv.at[2 + h],
        )
        for h in range(2)
    ]

    for h in range(2):
        first_halo[h][1]()
        src = lateral(ua, h)
        for pair in range(2):
            a = stencil(src, h, 4 + 2 * pair)
            b = stencil(src, h, 5 + 2 * pair)
            for t in range(8):
                lanes = slice(128 * t, 128 * t + 128)
                even, odd = swap(a[:, lanes], b[:, lanes])
                xs1[h, 2 * t, 8 * pair : 8 * pair + 8] = even
                xs1[h, 2 * t + 1, 8 * pair : 8 * pair + 8] = odd
        x1[h][0]()
        xr1[h, gx] = xs1[h, gx]

    def vertical(load, store):
        def forward(j, prev):
            for i in range(8):
                k = 8 * j + i
                prev = load(j, i) * inv_ref[k] + fa_ref[k] * prev
                fw[k] = prev
            return prev

        lax.fori_loop(0, 8, forward, zero_row)

        def backward(k, prev):
            j = 7 - k
            for i in range(7, -1, -1):
                prev = fw[8 * j + i] + fb_ref[8 * j + i] * prev
                store(j, i, prev)
            return prev

        lax.fori_loop(0, 8, backward, zero_row)

    z = gx // 2
    core = gx % 2

    def chip(off):
        return lax.rem(z + off + 8, 8)

    def o1_copy(h, peer, slot):
        return pltpu.make_async_remote_copy(
            src_ref=p_ref.at[h, peer],
            dst_ref=r1.at[h, slot],
            send_sem=o1_send.at[h, peer],
            recv_sem=o1_recv.at[h, slot],
            device_id={"gx": peer},
            device_id_type=pl.DeviceIdType.MESH,
        )

    def o4_copy(h, c, s, k, peer, slot):
        return pltpu.make_async_remote_copy(
            src_ref=u_ref.at[c, s, k, h],
            dst_ref=back.at[h, slot],
            send_sem=o4_send.at[h, peer],
            recv_sem=o4_recv.at[h, slot],
            device_id={"gx": peer},
            device_id_type=pl.DeviceIdType.MESH,
        )

    def peers(c, s, step):
        off = OFFSETS[c][s]
        if off == 0:
            step(1 - core, 2 * z + 1 - core)
        else:
            for k in range(2):
                step(k, 2 * chip(off) + k)

    o2 = [
        [
            exchange(
                lambda p, h=h, c=c: t2.at[h, p // 2, p % 2, c],
                lambda s, h=h, c=c: a_ref.at[h, c, s],
                "gy",
                gy,
                o2_send.at[h, c],
                o2_recv.at[h, c],
            )
            for c in range(4)
        ]
        for h in range(2)
    ]
    o3 = [
        exchange(
            lambda p, c=c: q_ref.at[c, p],
            lambda s, c=c: b_ref.at[c, s // 2, s % 2],
            "gy",
            gy,
            o3_send.at[c],
            o3_recv.at[c],
        )
        for c in range(4)
    ]

    for h in range(2):
        x1[h][1]()

        def load_column(j, i, h=h):
            return xr1[h, 2 * j + i // 4, pl.ds(i % 4, 4, stride=4), :]

        def store_column(j, i, value, h=h):
            sm[h, pl.ds(8 * j + i, 4, stride=64), :] = value

        vertical(load_column, store_column)
        s_hi, s_lo = split(jnp.concatenate([sm[h, 0:128], sm[h, 128:256]], axis=1))

        for c in range(4):
            for s in range(2):
                j = chip(OFFSETS[c][s])
                rows = pl.ds(pl.multiple_of(128 * j, 128), 128)
                value = dot3(w_hi[rows, :], w_lo[rows, :], s_hi, s_lo, ((1,), (1,)))
                p_ref[h, pl.ds(2 * j, 2)] = value.reshape(2, 8, 8, 128)
                peers(c, s, lambda k, peer: o1_copy(h, peer, gx).start())
        r1[h, gx] = p_ref[h, gx]

    top = lax.broadcasted_iota(jnp.int32, (8, 8, 128), 1) < 4

    def mix(a, b):
        return (
            jnp.where(top, a, pltpu.roll(b, 4, 1)),
            jnp.where(top, pltpu.roll(a, 4, 1), b),
        )

    def forward_chunk(h, c):
        for s in range(2):
            peers(c, s, lambda k, peer: o1_copy(h, peer, peer).wait_recv())
            j = chip(OFFSETS[c][s])
            even, odd = mix(r1[h, 2 * j], r1[h, 2 * j + 1])
            t2[h, :, 0, c, s] = even
            t2[h, :, 1, c, s] = odd
        o2[h][c][0]()
        a_ref[h, c, gy] = t2[h, gy // 2, gy % 2, c]

    def weigh(c):
        o2[0][c][1]()
        o2[1][c][1]()
        blocks = [a_ref[h, c].reshape(256, 128) for h in range(2)]
        hi, lo = split(jnp.concatenate(blocks, axis=1))
        value = dot3(hi, lo, e_hi[...], e_lo[...], ((1,), (0,)))
        for h in range(2):
            q_ref[c, :, h] = value[:, 128 * h : 128 * h + 128].reshape(N, 2, 8, 128)
        o3[c][0]()
        b_ref[c, gy // 2, gy % 2] = q_ref[c, gy]

    def return_chunk(c):
        o3[c][1]()
        for h in range(2):
            for s in range(2):
                even, odd = mix(b_ref[c, :, 0, h, s], b_ref[c, :, 1, h, s])
                u_ref[c, s, 0, h] = even
                u_ref[c, s, 1, h] = odd
        send_back(c, 0)

    def send_back(c, h):
        for s in range(2):
            peers(c, s, lambda k, peer: o4_copy(h, c, s, k, peer, gx).start())
            if OFFSETS[c][s] == 0:
                back[h, gx] = u_ref[c, s, core, h]

    for c in range(4):
        forward_chunk(0, c)
    forward_chunk(1, 0)
    forward_chunk(1, 1)
    weigh(0)
    forward_chunk(1, 2)
    weigh(1)
    return_chunk(0)
    forward_chunk(1, 3)
    weigh(2)
    return_chunk(1)
    weigh(3)
    return_chunk(2)
    return_chunk(3)
    for c in range(4):
        send_back(c, 1)

    for h in range(2):
        for c in range(4):
            for s in range(2):
                peers(c, s, lambda k, peer: o4_copy(h, c, s, k, peer, peer).wait_recv())
        b_hi, b_lo = split(back[h].reshape(1024, 128))
        spread = dot3(b_hi, b_lo, w_hi[...], w_lo[...], ((0,), (0,)))
        sp[h, 0:128] = spread[:, 0:128]
        sp[h, 128:256] = spread[:, 128:256]

        def load_spread(j, i, h=h):
            return sp[h, pl.ds(8 * j + i, 4, stride=64), :]

        def store_spread(j, i, value, h=h):
            xs2[h, 2 * j + i // 4, pl.ds(i % 4, 4, stride=4), :] = value

        vertical(load_spread, store_spread)
        x2[h][0]()
        xr2[h, gx] = xs2[h, gx]

    for h in range(2):
        x2[h][1]()
        for pair in range(2):
            rows = slice(8 * pair, 8 * pair + 8)
            for t in range(8):
                a, b = swap(xr2[h, 2 * t, rows], xr2[h, 2 * t + 1, rows])
                uc[h, 4 + 2 * pair, :, 128 * t : 128 * t + 128] = a
                uc[h, 5 + 2 * pair, :, 128 * t : 128 * t + 128] = b
        second_halo[h][0]()

    for h in range(2):
        second_halo[h][1]()
        second_halo[h][2]()
        src = lateral(uc, h)
        for r in range(4):
            tile = stencil(src, h, 4 + r)
            for v in range(2):
                for l in range(4):
                    k = 4 * v + l
                    image_ref[2 * h + v, l, r : r + 1, :] = tile[k : k + 1]

    def last(i, carry):
        pq, rq, qq = carry
        v, l = i // 4, i % 4
        d, r = dir_ref[v, l], res_ref[v, l]
        q = d + image_ref[v, l]
        image_ref[v, l] = q
        return pq + d * q, rq + r * q, qq + q * q

    sums = lax.fori_loop(0, 16, last, (zero_tile(), zero_tile(), zero_tile()))

    def fold(x):
        total = x[:, 0:128]
        for t in range(1, 8):
            total = total + x[:, 128 * t : 128 * t + 128]
        return jnp.sum(total, axis=0, keepdims=True)

    rows = [fold(x) for x in (rr, *sums)]
    part[...] = jnp.concatenate(rows + [jnp.zeros((4, 128), F32)], axis=0)
    g1 = exchange(lambda p: part, lambda s: gat1.at[s], "gx", gx, r_send.at[0], r_recv.at[0])
    g2 = exchange(lambda p: part2, lambda s: gat2.at[s], "gy", gy, r_send.at[1], r_recv.at[1])
    g1[0]()
    gat1[gx] = part[...]
    g1[1]()
    part2[...] = jnp.sum(gat1[...], axis=0)
    g2[0]()
    gat2[gy] = part2[...]
    g2[1]()
    total = jnp.sum(jnp.sum(gat2[...], axis=0), axis=1, keepdims=True)
    norm_now, curvature = total[0:1], total[1:2]
    cross, image_norm = total[2:3], total[3:4]
    alpha = norm_now / curvature
    norm_next = norm_now - 2.0 * alpha * cross + alpha * alpha * image_norm
    beta = norm_next / norm_now
    scal_ref[...] = jnp.concatenate(
        [jnp.broadcast_to(alpha, (4, 128)), jnp.broadcast_to(beta, (4, 128))], axis=0
    )

    for group in coef_halos:
        group[2]()
    for h in range(2):
        first_halo[h][2]()
        x1[h][2]()
        x2[h][2]()
        for c in range(4):
            o2[h][c][2]()
            for s in range(2):
                peers(c, s, lambda k, peer: o1_copy(h, peer, gx).wait_send())
                peers(c, s, lambda k, peer: o4_copy(h, c, s, k, peer, gx).wait_send())
    for c in range(4):
        o3[c][2]()
    g1[2]()
    g2[2]()


def update(image_ref, scal_ref, dir_ref, sol_ref, res_ref, sol_out, res_out, dir_out):
    alpha = scal_ref[0:1, 0:1]
    beta = scal_ref[4:5, 0:1]

    def each(i, carry):
        v, l = i // 4, i % 4
        d = dir_ref[v, l]
        r = res_ref[v, l] - alpha * image_ref[v, l]
        sol_out[v, l] = sol_ref[v, l] + alpha * d
        res_out[v, l] = r
        dir_out[v, l] = r + beta * d
        return carry

    lax.fori_loop(0, 16, each, 0)


def per_device(
    direction,
    solution,
    residual,
    north_coef,
    east_coef,
    ocean,
    vert_coef,
    obs_owner,
    obs_row,
    obs_col,
    obs_frac,
    error_inverse,
):
    vm = pltpu.VMEM
    dma = pltpu.SemaphoreType.DMA
    field = jax.ShapeDtypeStruct((4, 4, 4, 1024), F32)
    in_vmem = pl.BlockSpec(memory_space=pltpu.VMEM)
    level = vm((64, 4, 128), F32)
    wide = vm((2, 12, 8, 1024), F32)
    swap_buf = vm((2, N, 16, 128), F32)
    image, scal = pl.pallas_call(
        kernel,
        out_shape=(field, jax.ShapeDtypeStruct((8, 128), F32)),
        in_specs=[in_vmem] * 11,
        out_specs=(in_vmem,) * 2,
        scratch_shapes=[
            vm((2, 4, 8, 1024), F32),
            wide,
            wide,
            wide,
            vm((3, 4, 1024), F32),
            vm((3, 4, 1024), F32),
            vm((3, 4, 1024), jnp.int32),
            vm((12, 4, 8, 1024), F32),
            vm((512, 128), F32),
            level,
            level,
            level,
            level,
            level,
            vm((512, 256), BF16),
            vm((512, 256), BF16),
            vm((1024, 256), BF16),
            vm((1024, 256), BF16),
            vm((256, 256), BF16),
            vm((256, 256), BF16),
            swap_buf,
            swap_buf,
            vm((2, 256, 128), F32),
            vm((2, N, 8, 8, 128), F32),
            vm((2, N, 8, 8, 128), F32),
            vm((2, 8, 2, 4, 2, 8, 128), F32),
            vm((2, 4, N, 2, 8, 128), F32),
            vm((4, N, 2, 2, 8, 128), F32),
            vm((4, 8, 2, 2, 2, 8, 128), F32),
            vm((4, 2, 2, 2, 8, 8, 128), F32),
            vm((2, N, 8, 8, 128), F32),
            vm((2, 256, 128), F32),
            swap_buf,
            swap_buf,
            vm((8, 128), F32),
            vm((N, 8, 128), F32),
            vm((8, 128), F32),
            vm((N, 8, 128), F32),
            dma((14,)),
            dma((14,)),
            dma((4, N)),
            dma((4, N)),
            dma((2, N)),
            dma((2, N)),
            dma((2, 4, N)),
            dma((2, 4, N)),
            dma((4, N)),
            dma((4, N)),
            dma((2, N)),
            dma((2, N)),
            dma((2, N)),
            dma((2, N)),
        ],
        compiler_params=pltpu.CompilerParams(collective_id=0, has_side_effects=True),
        name="cg_step",
    )(
        direction,
        residual,
        north_coef,
        east_coef,
        ocean,
        vert_coef,
        obs_owner.reshape(1, 512),
        obs_row.reshape(1, 512),
        obs_col.reshape(1, 512),
        obs_frac.reshape(2, 512),
        error_inverse.reshape(256, 256),
    )
    return pl.pallas_call(
        update,
        out_shape=(field,) * 3,
        in_specs=[in_vmem] * 5,
        out_specs=(in_vmem,) * 3,
        name="cg_update",
    )(image, scal, direction, solution, residual)


def solution(mesh):
    field = P(None, "gx", "gy", None)
    in_specs = (
        field,
        field,
        field,
        P("gy", None),
        P("gy", None),
        P("gy", None),
        P(None, "gy", "gx"),
        P("gy", "gx", None, None),
        P("gy", "gx", None),
        P("gy", "gx", None),
        P("gy", "gx", None, None),
        P("gy", "gx", None, None),
    )
    return jax.shard_map(
        per_device, mesh=mesh, in_specs=in_specs, out_specs=(field,) * 3, check_vma=False
    )
```

```python
import functools

import jax
import jax.numpy as jnp
from jax import lax
from jax.experimental import pallas as pl
from jax.experimental.pallas import tpu as pltpu
from jax.sharding import PartitionSpec as P

NSTEP = 4
N = 16
F32 = jnp.float32
BF16 = jnp.bfloat16


def split(x):
    hi = x.astype(BF16)
    lo = (x - hi.astype(F32)).astype(BF16)
    return hi, lo


def dot(a, b, dims):
    return lax.dot_general(a, b, (dims, ((), ())), preferred_element_type=F32)


def dot3(a_hi, a_lo, b_hi, b_lo, dims):
    return dot(a_hi, b_hi, dims) + (dot(a_hi, b_lo, dims) + dot(a_lo, b_hi, dims))


def exchange(src, dst, axis, me, send_sem, recv_sem):
    def copy(peer, slot):
        return pltpu.make_async_remote_copy(
            src_ref=src(peer),
            dst_ref=dst(slot),
            send_sem=send_sem.at[peer],
            recv_sem=recv_sem.at[slot],
            device_id={axis: peer},
            device_id_type=pl.DeviceIdType.MESH,
        )

    def each(step):
        def body(d, carry):
            step(lax.rem(me + d, N))
            return carry

        lax.fori_loop(1, N, body, 0)

    def start():
        each(lambda peer: copy(peer, me).start())

    def wait_recv():
        each(lambda peer: copy(peer, peer).wait_recv())

    def wait_send():
        each(lambda peer: copy(peer, peer).wait_send())

    return start, wait_recv, wait_send


OFFSETS = ((1, -1), (2, -2), (0, 4), (3, -3))


def kernel(
    dir_ref,
    res_ref,
    north_ref,
    east_ref,
    ocean_ref,
    vert_ref,
    own_ref,
    row_ref,
    col_ref,
    frac_ref,
    err_ref,
    image_ref,
    scal_ref,
    dt,
    ua,
    ub,
    uc,
    hn,
    he,
    ho,
    cf,
    obs_ref,
    vb,
    inv_ref,
    fa_ref,
    fb_ref,
    fw,
    c_hi,
    c_lo,
    w_hi,
    w_lo,
    wt_hi,
    wt_lo,
    e_hi,
    e_lo,
    xs1,
    xr1,
    sm,
    p_ref,
    r1,
    t2,
    a_ref,
    q_ref,
    b_ref,
    u_ref,
    back,
    sp,
    xs2,
    xr2,
    part,
    gat1,
    part2,
    gat2,
    hs_send,
    hs_recv,
    x_send,
    x_recv,
    o1_send,
    o1_recv,
    o2_send,
    o2_recv,
    o3_send,
    o3_recv,
    o4_send,
    o4_recv,
    r_send,
    r_recv,
):
    gy = lax.axis_index("gy")
    gx = lax.axis_index("gx")

    barrier = pltpu.get_barrier_semaphore()

    def greet(d, carry):
        pl.semaphore_signal(
            barrier,
            inc=1,
            device_id={"gx": lax.rem(gx + d, N)},
            device_id_type=pl.DeviceIdType.MESH,
        )
        pl.semaphore_signal(
            barrier,
            inc=1,
            device_id={"gy": lax.rem(gy + d, N)},
            device_id_type=pl.DeviceIdType.MESH,
        )
        return carry

    lax.fori_loop(1, N, greet, 0)

    for h in range(2):
        for r in range(4):
            rows = [dir_ref[2 * h + v, l, r : r + 1, :] for v in range(2) for l in range(4)]
            tile = jnp.concatenate(rows, axis=0)
            dt[h, r] = tile
            ua[h, 4 + r] = tile

    owner_row = own_ref[...].astype(F32)
    table = jnp.concatenate(
        [
            owner_row,
            row_ref[...].astype(F32),
            col_ref[...].astype(F32),
            frac_ref[...],
            jnp.zeros((123, 512), F32),
        ],
        axis=0,
    )
    for g in range(4):
        obs_ref[128 * g : 128 * g + 128, :] = table[:, 128 * g : 128 * g + 128].T
    lane512 = lax.broadcasted_iota(jnp.int32, (64, 512), 1)
    sub512 = lax.broadcasted_iota(jnp.int32, (64, 512), 0)
    cell = lax.broadcasted_iota(jnp.int32, (64, 256), 1)
    cell_row = (cell // 64).astype(F32)
    cell_lon = (cell % 64).astype(F32)

    def obs_group(g, rank):
        rows = pl.ds(pl.multiple_of(64 * g, 64), 64)
        block = obs_ref[rows, :]
        o, r, c = block[:, 0:1], block[:, 1:2], block[:, 2:3]
        fr, fc = block[:, 3:4], block[:, 4:5]
        lat = jnp.where(cell_row == r, 1.0 - fr, jnp.where(cell_row == r + 1.0, fr, 0.0))
        lon = jnp.where(cell_lon == c, 1.0 - fc, jnp.where(cell_lon == c + 1.0, fc, 0.0))
        hi, lo = split(lat * lon)
        c_hi[rows, :] = hi
        c_lo[rows, :] = lo
        same = (o == owner_row) & (sub512 + 64 * g < lane512)
        return rank + jnp.sum(jnp.where(same, 1.0, 0.0), axis=0, keepdims=True)

    rank = lax.fori_loop(0, 8, obs_group, jnp.zeros((1, 512), F32))
    owner_int = own_ref[...]
    slot = ((owner_int % N) * N + owner_int // N) * 4 + rank.astype(jnp.int32)

    def slot_group(g, carry):
        base = pl.multiple_of(256 * g, 256)
        sub = lax.broadcasted_iota(jnp.int32, (256, 512), 0) + base
        hot = jnp.where(sub == slot, 1.0, 0.0).astype(BF16)
        rows = pl.ds(base, 256)
        for src, dst, dst_t in ((c_hi, w_hi, wt_hi), (c_lo, w_lo, wt_lo)):
            value = dot(hot, src[...], ((1,), (0,)))
            dst[rows, :] = value.astype(BF16)
            dst_t[:, rows] = value.T.astype(BF16)
        return carry

    lax.fori_loop(0, 4, slot_group, 0)
    hi, lo = split(err_ref[...])
    e_hi[...] = hi
    e_lo[...] = lo

    pl.semaphore_wait(barrier, 2 * (N - 1))

    def halo_copy(src, dst, sem, toward):
        return pltpu.make_async_remote_copy(
            src_ref=src,
            dst_ref=dst,
            send_sem=hs_send.at[sem],
            recv_sem=hs_recv.at[sem],
            device_id={"gy": toward},
            device_id_type=pl.DeviceIdType.MESH,
        )

    def halo(src, buf, sem):
        def up():
            return halo_copy(src, buf(0), sem, gy + 1)

        def down():
            return halo_copy(src, buf(2), sem + 1, gy - 1)

        def start():
            @pl.when(gy < N - 1)
            def _():
                up().start()

            @pl.when(gy > 0)
            def _():
                down().start()

        def wait_recv():
            @pl.when(gy > 0)
            def _():
                up().wait_recv()

            @pl.when(gy < N - 1)
            def _():
                down().wait_recv()

        def wait_send():
            @pl.when(gy < N - 1)
            def _():
                up().wait_send()

            @pl.when(gy > 0)
            def _():
                down().wait_send()

        return start, wait_recv, wait_send

    coef_halos = [
        halo(north_ref, lambda b: hn.at[b], 0),
        halo(east_ref, lambda b: he.at[b], 2),
        halo(ocean_ref, lambda b: ho.at[b], 4),
    ]
    first_halo = [
        halo(dt.at[h], lambda b, h=h: ua.at[h, pl.ds(4 * b, 4)], 6 + 2 * h) for h in range(2)
    ]
    second_halo = [
        halo(uc.at[h, pl.ds(4, 4)], lambda b, h=h: uc.at[h, pl.ds(4 * b, 4)], 10 + 2 * h)
        for h in range(2)
    ]
    for group in coef_halos:
        group[0]()
    first_halo[0][0]()
    first_halo[1][0]()

    @pl.when(gy == 0)
    def _():
        hn[0] = jnp.zeros((4, 1024), F32)
        he[0] = jnp.zeros((4, 1024), F32)
        ho[0] = jnp.zeros((4, 1024), jnp.int32)
        for h in range(2):
            ua[h, pl.ds(0, 4)] = jnp.zeros((4, 8, 1024), F32)
            uc[h, pl.ds(0, 4)] = jnp.zeros((4, 8, 1024), F32)

    @pl.when(gy == N - 1)
    def _():
        hn[2] = jnp.zeros((4, 1024), F32)
        he[2] = jnp.zeros((4, 1024), F32)
        ho[2] = jnp.zeros((4, 1024), jnp.int32)
        for h in range(2):
            ua[h, pl.ds(8, 4)] = jnp.zeros((4, 8, 1024), F32)
            uc[h, pl.ds(8, 4)] = jnp.zeros((4, 8, 1024), F32)

    hn[1] = north_ref[...]
    he[1] = east_ref[...]
    ho[1] = ocean_ref[...]

    def spread_rows(j, carry):
        for i in range(8):
            v = vert_ref[8 * j + i]
            left = jnp.concatenate([v[0:1], v[0:1], v[2:3], v[2:3]], axis=0)
            right = jnp.concatenate([v[1:2], v[1:2], v[3:4], v[3:4]], axis=0)
            vb[8 * j + i] = jnp.concatenate([left, right], axis=1)
        return carry

    lax.fori_loop(0, 8, spread_rows, 0)

    def factor_row(i, carry):
        v_prev, up_prev = carry
        v = vb[i]
        diagonal = 1.0 + v + v_prev + v_prev * up_prev
        inverse = 1.0 / diagonal
        ratio = v * inverse
        inv_ref[i] = inverse
        fa_ref[i] = v_prev * inverse
        fb_ref[i] = ratio
        return v, -ratio

    zero_row = jnp.zeros((4, 128), F32)
    lax.fori_loop(0, 64, factor_row, (zero_row, zero_row))

    def zero_tile():
        return jnp.zeros((4, 1024), F32)

    def rr_group(i, acc):
        x = res_ref[i // 4, i % 4]
        return acc + x * x

    rr = lax.fori_loop(0, 16, rr_group, zero_tile())

    for group in coef_halos:
        group[1]()

    def coef_row(i, q):
        buf = (hn, he, ho)[q]
        return buf[i // 4, i % 4 : i % 4 + 1, :].astype(F32)

    fn_prev = jnp.zeros((1, 1024), F32)
    for i in range(12):
        m = coef_row(i, 2)
        if i < 11:
            fn = coef_row(i, 0) * m * coef_row(i + 1, 2)
        else:
            fn = jnp.zeros((1, 1024), F32)
        fe = coef_row(i, 1) * m * pltpu.roll(m, 1023, 1)
        fw_e = pltpu.roll(fe, 1, 1)
        centre = m - fn - fn_prev - fe - fw_e
        for q, value in enumerate((centre, fn, fe, fw_e)):
            cf[i, q] = jnp.broadcast_to(value, (8, 1024))
        fn_prev = fn

    def stencil(src, h, i):
        u = src[h, i]
        return (
            cf[i, 0] * u
            + cf[i, 1] * src[h, i + 1]
            + cf[i - 1, 1] * src[h, i - 1]
            + cf[i, 2] * pltpu.roll(u, 1023, 1)
            + cf[i, 3] * pltpu.roll(u, 1, 1)
        )

    def lateral(buf, h):
        src, dst = buf, ub
        for step in range(NSTEP - 1):

            for i in range(1 + step, 11 - step):
                dst[h, i] = stencil(src, h, i)
            src, dst = dst, src
        return src

    low = lax.broadcasted_iota(jnp.int32, (8, 128), 1) < 64

    def swap(a, b):
        return (
            jnp.where(low, a, pltpu.roll(b, 64, 1)),
            jnp.where(low, pltpu.roll(a, 64, 1), b),
        )

    x1 = [
        exchange(
            lambda p, h=h: xs1.at[h, p],
            lambda s, h=h: xr1.at[h, s],
            "gx",
            gx,
            x_send.at[h],
            x_recv.at[h],
        )
        for h in range(2)
    ]
    x2 = [
        exchange(
            lambda p, h=h: xs2.at[h, p],
            lambda s, h=h: xr2.at[h, s],
            "gx",
            gx,
            x_send.at[2 + h],
            x_recv.at[2 + h],
        )
        for h in range(2)
    ]

    for h in range(2):
        first_halo[h][1]()
        src = lateral(ua, h)
        for pair in range(2):
            a = stencil(src, h, 4 + 2 * pair)
            b = stencil(src, h, 5 + 2 * pair)
            for t in range(8):
                lanes = slice(128 * t, 128 * t + 128)
                even, odd = swap(a[:, lanes], b[:, lanes])
                xs1[h, 2 * t, 8 * pair : 8 * pair + 8] = even
                xs1[h, 2 * t + 1, 8 * pair : 8 * pair + 8] = odd
        x1[h][0]()
        xr1[h, gx] = xs1[h, gx]

    def vertical(load, store):
        def forward(j, prev):
            for i in range(8):
                k = 8 * j + i
                prev = load(j, i) * inv_ref[k] + fa_ref[k] * prev
                fw[k] = prev
            return prev

        lax.fori_loop(0, 8, forward, zero_row)

        def backward(k, prev):
            j = 7 - k
            for i in range(7, -1, -1):
                prev = fw[8 * j + i] + fb_ref[8 * j + i] * prev
                store(j, i, prev)
            return prev

        lax.fori_loop(0, 8, backward, zero_row)

    z = gx // 2
    core = gx % 2

    def chip(off):
        return lax.rem(z + off + 8, 8)

    def o1_copy(h, peer, slot):
        return pltpu.make_async_remote_copy(
            src_ref=p_ref.at[h, peer],
            dst_ref=r1.at[h, slot],
            send_sem=o1_send.at[h, peer],
            recv_sem=o1_recv.at[h, slot],
            device_id={"gx": peer},
            device_id_type=pl.DeviceIdType.MESH,
        )

    def o4_copy(h, c, s, k, peer, slot):
        return pltpu.make_async_remote_copy(
            src_ref=u_ref.at[c, s, k, h],
            dst_ref=back.at[h, slot],
            send_sem=o4_send.at[h, peer],
            recv_sem=o4_recv.at[h, slot],
            device_id={"gx": peer},
            device_id_type=pl.DeviceIdType.MESH,
        )

    def peers(c, s, step):
        off = OFFSETS[c][s]
        if off == 0:
            step(1 - core, 2 * z + 1 - core)
        else:
            for k in range(2):
                step(k, 2 * chip(off) + k)

    o2 = [
        exchange(
            lambda p, c=c: t2.at[p // 2, p % 2, c],
            lambda s, c=c: a_ref.at[c, s],
            "gy",
            gy,
            o2_send.at[c],
            o2_recv.at[c],
        )
        for c in range(4)
    ]
    o3 = [
        exchange(
            lambda p, c=c: q_ref.at[c, p],
            lambda s, c=c: b_ref.at[c, s // 2, s % 2],
            "gy",
            gy,
            o3_send.at[c],
            o3_recv.at[c],
        )
        for c in range(4)
    ]

    def columns(h):
        x1[h][1]()

        def load_column(j, i):
            return xr1[h, 2 * j + i // 4, pl.ds(i % 4, 4, stride=4), :]

        def store_column(j, i, value):
            sm[h, pl.ds(8 * j + i, 4, stride=64), :] = value

        vertical(load_column, store_column)
        return split(jnp.concatenate([sm[h, 0:128], sm[h, 128:256]], axis=1))

    def profile(h, c, smoothed):
        for s in range(2):
            j = chip(OFFSETS[c][s])
            rows = pl.ds(pl.multiple_of(128 * j, 128), 128)
            value = dot3(w_hi[rows, :], w_lo[rows, :], *smoothed, ((1,), (1,)))
            p_ref[h, pl.ds(2 * j, 2)] = value.reshape(2, 8, 8, 128)
            peers(c, s, lambda k, peer: o1_copy(h, peer, gx).start())

    smoothed_0 = columns(0)
    profile(0, 0, smoothed_0)
    smoothed_1 = columns(1)
    profile(1, 0, smoothed_1)
    for c in range(1, 4):
        profile(0, c, smoothed_0)
        profile(1, c, smoothed_1)
    for h in range(2):
        r1[h, gx] = p_ref[h, gx]

    top = lax.broadcasted_iota(jnp.int32, (8, 8, 128), 1) < 4

    def mix(a, b):
        return (
            jnp.where(top, a, pltpu.roll(b, 4, 1)),
            jnp.where(top, pltpu.roll(a, 4, 1), b),
        )

    def forward_chunk(c):
        for h in range(2):
            for s in range(2):
                peers(c, s, lambda k, peer: o1_copy(h, peer, peer).wait_recv())
                j = chip(OFFSETS[c][s])
                even, odd = mix(r1[h, 2 * j], r1[h, 2 * j + 1])
                t2[:, 0, c, h, s] = even
                t2[:, 1, c, h, s] = odd
        o2[c][0]()
        a_ref[c, gy] = t2[gy // 2, gy % 2, c]

    def weigh(c):
        o2[c][1]()
        blocks = [a_ref[c, :, h].reshape(256, 128) for h in range(2)]
        hi, lo = split(jnp.concatenate(blocks, axis=1))
        value = dot3(hi, lo, e_hi[...], e_lo[...], ((1,), (0,)))
        for h in range(2):
            q_ref[c, :, h] = value[:, 128 * h : 128 * h + 128].reshape(N, 2, 8, 128)
        o3[c][0]()
        b_ref[c, gy // 2, gy % 2] = q_ref[c, gy]

    def return_chunk(c):
        o3[c][1]()
        for h in range(2):
            for s in range(2):
                even, odd = mix(b_ref[c, :, 0, h, s], b_ref[c, :, 1, h, s])
                u_ref[c, s, 0, h] = even
                u_ref[c, s, 1, h] = odd

    def send_back(c, h):
        for s in range(2):
            peers(c, s, lambda k, peer: o4_copy(h, c, s, k, peer, gx).start())
            if OFFSETS[c][s] == 0:
                back[h, gx] = u_ref[c, s, core, h]

    def back_chunk(c):
        return_chunk(c)
        for h in range(2):
            send_back(c, h)

    forward_chunk(0)
    forward_chunk(1)
    weigh(0)
    forward_chunk(2)
    weigh(1)
    back_chunk(0)
    forward_chunk(3)
    weigh(2)
    back_chunk(1)
    weigh(3)
    back_chunk(2)
    back_chunk(3)

    for h in range(2):
        spread = jnp.zeros((256, 128), F32)
        for c in range(4):
            for s in range(2):
                peers(c, s, lambda k, peer: o4_copy(h, c, s, k, peer, peer).wait_recv())
                j = chip(OFFSETS[c][s])
                cols = pl.ds(pl.multiple_of(128 * j, 128), 128)
                b_hi, b_lo = split(back[h, pl.ds(2 * j, 2)].reshape(128, 128))
                spread = spread + dot3(wt_hi[:, cols], wt_lo[:, cols], b_hi, b_lo, ((1,), (0,)))
        sp[h, 0:128] = spread[0:128].T
        sp[h, 128:256] = spread[128:256].T

        def load_spread(j, i, h=h):
            return sp[h, pl.ds(8 * j + i, 4, stride=64), :]

        def store_spread(j, i, value, h=h):
            xs2[h, 2 * j + i // 4, pl.ds(i % 4, 4, stride=4), :] = value

        vertical(load_spread, store_spread)
        x2[h][0]()
        xr2[h, gx] = xs2[h, gx]

    for h in range(2):
        x2[h][1]()
        for pair in range(2):
            rows = slice(8 * pair, 8 * pair + 8)
            for t in range(8):
                a, b = swap(xr2[h, 2 * t, rows], xr2[h, 2 * t + 1, rows])
                uc[h, 4 + 2 * pair, :, 128 * t : 128 * t + 128] = a
                uc[h, 5 + 2 * pair, :, 128 * t : 128 * t + 128] = b
        second_halo[h][0]()

    for h in range(2):
        second_halo[h][1]()
        second_halo[h][2]()
        src = lateral(uc, h)
        for r in range(4):
            tile = stencil(src, h, 4 + r)
            for v in range(2):
                for l in range(4):
                    k = 4 * v + l
                    image_ref[2 * h + v, l, r : r + 1, :] = tile[k : k + 1]

    def last(i, carry):
        pq, rq, qq = carry
        v, l = i // 4, i % 4
        d, r = dir_ref[v, l], res_ref[v, l]
        q = d + image_ref[v, l]
        image_ref[v, l] = q
        return pq + d * q, rq + r * q, qq + q * q

    sums = lax.fori_loop(0, 16, last, (zero_tile(), zero_tile(), zero_tile()))

    def fold(x):
        total = x[:, 0:128]
        for t in range(1, 8):
            total = total + x[:, 128 * t : 128 * t + 128]
        return jnp.sum(total, axis=0, keepdims=True)

    rows = [fold(x) for x in (rr, *sums)]
    part[...] = jnp.concatenate(rows, axis=0)
    g1 = exchange(lambda p: part, lambda s: gat1.at[s], "gx", gx, r_send.at[0], r_recv.at[0])
    g2 = exchange(lambda p: part2, lambda s: gat2.at[s], "gy", gy, r_send.at[1], r_recv.at[1])
    g1[0]()
    gat1[gx] = part[...]
    for group in coef_halos:
        group[2]()
    for h in range(2):
        first_halo[h][2]()
        x1[h][2]()
        for c in range(4):
            for s in range(2):
                peers(c, s, lambda k, peer: o1_copy(h, peer, gx).wait_send())
    g1[1]()
    part2[...] = jnp.sum(gat1[...], axis=0)
    g2[0]()
    gat2[gy] = part2[...]
    for h in range(2):
        x2[h][2]()
        for c in range(4):
            for s in range(2):
                peers(c, s, lambda k, peer: o4_copy(h, c, s, k, peer, gx).wait_send())
    for c in range(4):
        o2[c][2]()
        o3[c][2]()
    g1[2]()
    g2[1]()
    total = jnp.sum(jnp.sum(gat2[...], axis=0), axis=1, keepdims=True)
    norm_now, curvature = total[0:1], total[1:2]
    cross, image_norm = total[2:3], total[3:4]
    alpha = norm_now / curvature
    norm_next = norm_now - 2.0 * alpha * cross + alpha * alpha * image_norm
    beta = norm_next / norm_now
    scal_ref[...] = jnp.concatenate(
        [jnp.broadcast_to(alpha, (4, 128)), jnp.broadcast_to(beta, (4, 128))], axis=0
    )
    g2[2]()


def update(image_ref, scal_ref, dir_ref, sol_ref, res_ref, sol_out, res_out, dir_out):
    alpha = scal_ref[0:1, 0:1]
    beta = scal_ref[4:5, 0:1]

    for l in range(4):
        d = dir_ref[0, l]
        r = res_ref[0, l] - alpha * image_ref[0, l]
        sol_out[0, l] = sol_ref[0, l] + alpha * d
        res_out[0, l] = r
        dir_out[0, l] = r + beta * d


def per_device(
    direction,
    solution,
    residual,
    north_coef,
    east_coef,
    ocean,
    vert_coef,
    obs_owner,
    obs_row,
    obs_col,
    obs_frac,
    error_inverse,
):
    vm = pltpu.VMEM
    dma = pltpu.SemaphoreType.DMA
    field = jax.ShapeDtypeStruct((4, 4, 4, 1024), F32)
    in_vmem = pl.BlockSpec(memory_space=pltpu.VMEM)
    block = pl.BlockSpec((1, 4, 4, 1024), lambda i: (i, 0, 0, 0))
    level = vm((64, 4, 128), F32)
    wide = vm((2, 12, 8, 1024), F32)
    swap_buf = vm((2, N, 16, 128), F32)
    image, scal = pl.pallas_call(
        kernel,
        out_shape=(field, jax.ShapeDtypeStruct((8, 128), F32)),
        in_specs=[in_vmem] * 11,
        out_specs=(in_vmem,) * 2,
        scratch_shapes=[
            vm((2, 4, 8, 1024), F32),
            wide,
            wide,
            wide,
            vm((3, 4, 1024), F32),
            vm((3, 4, 1024), F32),
            vm((3, 4, 1024), jnp.int32),
            vm((12, 4, 8, 1024), F32),
            vm((512, 128), F32),
            level,
            level,
            level,
            level,
            level,
            vm((512, 256), BF16),
            vm((512, 256), BF16),
            vm((1024, 256), BF16),
            vm((1024, 256), BF16),
            vm((256, 1024), BF16),
            vm((256, 1024), BF16),
            vm((256, 256), BF16),
            vm((256, 256), BF16),
            swap_buf,
            swap_buf,
            vm((2, 256, 128), F32),
            vm((2, N, 8, 8, 128), F32),
            vm((2, N, 8, 8, 128), F32),
            vm((8, 2, 4, 2, 2, 8, 128), F32),
            vm((4, N, 2, 2, 8, 128), F32),
            vm((4, N, 2, 2, 8, 128), F32),
            vm((4, 8, 2, 2, 2, 8, 128), F32),
            vm((4, 2, 2, 2, 8, 8, 128), F32),
            vm((2, N, 8, 8, 128), F32),
            vm((2, 256, 128), F32),
            swap_buf,
            swap_buf,
            vm((4, 128), F32),
            vm((N, 4, 128), F32),
            vm((4, 128), F32),
            vm((N, 4, 128), F32),
            dma((14,)),
            dma((14,)),
            dma((4, N)),
            dma((4, N)),
            dma((2, N)),
            dma((2, N)),
            dma((4, N)),
            dma((4, N)),
            dma((4, N)),
            dma((4, N)),
            dma((2, N)),
            dma((2, N)),
            dma((2, N)),
            dma((2, N)),
        ],
        compiler_params=pltpu.CompilerParams(collective_id=0, has_side_effects=True),
        name="cg_step",
    )(
        direction,
        residual,
        north_coef,
        east_coef,
        ocean,
        vert_coef,
        obs_owner.reshape(1, 512),
        obs_row.reshape(1, 512),
        obs_col.reshape(1, 512),
        obs_frac.reshape(2, 512),
        error_inverse.reshape(256, 256),
    )
    return pl.pallas_call(
        update,
        out_shape=(field,) * 3,
        grid=(4,),
        in_specs=[block, in_vmem, block, block, block],
        out_specs=(block,) * 3,
        name="cg_update",
    )(image, scal, direction, solution, residual)


def solution(mesh):
    field = P(None, "gx", "gy", None)
    in_specs = (
        field,
        field,
        field,
        P("gy", None),
        P("gy", None),
        P("gy", None),
        P(None, "gy", "gx"),
        P("gy", "gx", None, None),
        P("gy", "gx", None),
        P("gy", "gx", None),
        P("gy", "gx", None, None),
        P("gy", "gx", None, None),
    )
    return jax.shard_map(
        per_device, mesh=mesh, in_specs=in_specs, out_specs=(field,) * 3, check_vma=False
    )
```

```python
import functools

import jax
import jax.numpy as jnp
from jax import lax
from jax.experimental import pallas as pl
from jax.experimental.pallas import tpu as pltpu
from jax.sharding import PartitionSpec as P

NSTEP = 4
N = 16
F32 = jnp.float32
BF16 = jnp.bfloat16


def split(x):
    hi = x.astype(BF16)
    lo = (x - hi.astype(F32)).astype(BF16)
    return hi, lo


def dot(a, b, dims):
    return lax.dot_general(a, b, (dims, ((), ())), preferred_element_type=F32)


def dot3(a_hi, a_lo, b_hi, b_lo, dims):
    return dot(a_hi, b_hi, dims) + (dot(a_hi, b_lo, dims) + dot(a_lo, b_hi, dims))


def exchange(src, dst, axis, me, send_sem, recv_sem):
    def copy(peer, slot):
        return pltpu.make_async_remote_copy(
            src_ref=src(peer),
            dst_ref=dst(slot),
            send_sem=send_sem.at[peer],
            recv_sem=recv_sem.at[slot],
            device_id={axis: peer},
            device_id_type=pl.DeviceIdType.MESH,
        )

    def each(step):
        def body(d, carry):
            step(lax.rem(me + d, N))
            return carry

        lax.fori_loop(1, N, body, 0)

    def start():
        each(lambda peer: copy(peer, me).start())

    def wait_recv():
        each(lambda peer: copy(peer, peer).wait_recv())

    def wait_send():
        each(lambda peer: copy(peer, peer).wait_send())

    return start, wait_recv, wait_send


OFFSETS = ((0, 4), (2, -2), (3, -3), (1, -1))


def kernel(
    dir_ref,
    res_ref,
    north_ref,
    east_ref,
    ocean_ref,
    vert_ref,
    own_ref,
    row_ref,
    col_ref,
    frac_ref,
    err_ref,
    image_ref,
    scal_ref,
    dt,
    ua,
    ub,
    uc,
    hn,
    he,
    ho,
    cf,
    obs_ref,
    vb,
    inv_ref,
    fa_ref,
    fb_ref,
    fw,
    c_hi,
    c_lo,
    w_hi,
    w_lo,
    wt_hi,
    wt_lo,
    e_hi,
    e_lo,
    xs1,
    xr1,
    sm,
    p_ref,
    r1,
    t2,
    a_ref,
    q_ref,
    b_ref,
    u_ref,
    back,
    sp,
    xs2,
    xr2,
    part,
    gat1,
    part2,
    gat2,
    hs_send,
    hs_recv,
    x_send,
    x_recv,
    o1_send,
    o1_recv,
    o2_send,
    o2_recv,
    o3_send,
    o3_recv,
    o4_send,
    o4_recv,
    r_send,
    r_recv,
):
    gy = lax.axis_index("gy")
    gx = lax.axis_index("gx")

    barrier = pltpu.get_barrier_semaphore()

    def greet(d, carry):
        pl.semaphore_signal(
            barrier,
            inc=1,
            device_id={"gx": lax.rem(gx + d, N)},
            device_id_type=pl.DeviceIdType.MESH,
        )
        pl.semaphore_signal(
            barrier,
            inc=1,
            device_id={"gy": lax.rem(gy + d, N)},
            device_id_type=pl.DeviceIdType.MESH,
        )
        return carry

    lax.fori_loop(1, N, greet, 0)

    for h in range(2):
        for r in range(4):
            rows = [dir_ref[2 * h + v, l, r : r + 1, :] for v in range(2) for l in range(4)]
            tile = jnp.concatenate(rows, axis=0)
            dt[h, r] = tile
            ua[h, 4 + r] = tile

    owner_row = own_ref[...].astype(F32)
    table = jnp.concatenate(
        [
            owner_row,
            row_ref[...].astype(F32),
            col_ref[...].astype(F32),
            frac_ref[...],
            jnp.zeros((123, 512), F32),
        ],
        axis=0,
    )
    for g in range(4):
        obs_ref[128 * g : 128 * g + 128, :] = table[:, 128 * g : 128 * g + 128].T
    lane512 = lax.broadcasted_iota(jnp.int32, (64, 512), 1)
    sub512 = lax.broadcasted_iota(jnp.int32, (64, 512), 0)
    cell = lax.broadcasted_iota(jnp.int32, (64, 256), 1)
    cell_row = (cell // 64).astype(F32)
    cell_lon = (cell % 64).astype(F32)

    def obs_group(g, rank):
        rows = pl.ds(pl.multiple_of(64 * g, 64), 64)
        block = obs_ref[rows, :]
        o, r, c = block[:, 0:1], block[:, 1:2], block[:, 2:3]
        fr, fc = block[:, 3:4], block[:, 4:5]
        lat = jnp.where(cell_row == r, 1.0 - fr, jnp.where(cell_row == r + 1.0, fr, 0.0))
        lon = jnp.where(cell_lon == c, 1.0 - fc, jnp.where(cell_lon == c + 1.0, fc, 0.0))
        hi, lo = split(lat * lon)
        c_hi[rows, :] = hi
        c_lo[rows, :] = lo
        same = (o == owner_row) & (sub512 + 64 * g < lane512)
        return rank + jnp.sum(jnp.where(same, 1.0, 0.0), axis=0, keepdims=True)

    rank = lax.fori_loop(0, 8, obs_group, jnp.zeros((1, 512), F32))
    owner_int = own_ref[...]
    slot = ((owner_int % N) * N + owner_int // N) * 4 + rank.astype(jnp.int32)

    def slot_group(g, carry):
        base = pl.multiple_of(256 * g, 256)
        sub = lax.broadcasted_iota(jnp.int32, (256, 512), 0) + base
        hot = jnp.where(sub == slot, 1.0, 0.0).astype(BF16)
        rows = pl.ds(base, 256)
        for src, dst, dst_t in ((c_hi, w_hi, wt_hi), (c_lo, w_lo, wt_lo)):
            value = dot(hot, src[...], ((1,), (0,)))
            dst[rows, :] = value.astype(BF16)
            dst_t[:, rows] = value.T.astype(BF16)
        return carry

    lax.fori_loop(0, 4, slot_group, 0)
    hi, lo = split(err_ref[...])
    e_hi[...] = hi
    e_lo[...] = lo

    pl.semaphore_wait(barrier, 2 * (N - 1))

    def halo_copy(src, dst, sem, toward):
        return pltpu.make_async_remote_copy(
            src_ref=src,
            dst_ref=dst,
            send_sem=hs_send.at[sem],
            recv_sem=hs_recv.at[sem],
            device_id={"gy": toward},
            device_id_type=pl.DeviceIdType.MESH,
        )

    def halo(src, buf, sem):
        def up():
            return halo_copy(src, buf(0), sem, gy + 1)

        def down():
            return halo_copy(src, buf(2), sem + 1, gy - 1)

        def start():
            @pl.when(gy < N - 1)
            def _():
                up().start()

            @pl.when(gy > 0)
            def _():
                down().start()

        def wait_recv():
            @pl.when(gy > 0)
            def _():
                up().wait_recv()

            @pl.when(gy < N - 1)
            def _():
                down().wait_recv()

        def wait_send():
            @pl.when(gy < N - 1)
            def _():
                up().wait_send()

            @pl.when(gy > 0)
            def _():
                down().wait_send()

        return start, wait_recv, wait_send

    coef_halos = [
        halo(north_ref, lambda b: hn.at[b], 0),
        halo(east_ref, lambda b: he.at[b], 2),
        halo(ocean_ref, lambda b: ho.at[b], 4),
    ]
    first_halo = [
        halo(dt.at[h], lambda b, h=h: ua.at[h, pl.ds(4 * b, 4)], 6 + 2 * h) for h in range(2)
    ]
    second_halo = [
        halo(uc.at[h, pl.ds(4, 4)], lambda b, h=h: uc.at[h, pl.ds(4 * b, 4)], 10 + 2 * h)
        for h in range(2)
    ]
    for group in coef_halos:
        group[0]()
    first_halo[0][0]()
    first_halo[1][0]()

    @pl.when(gy == 0)
    def _():
        hn[0] = jnp.zeros((4, 1024), F32)
        he[0] = jnp.zeros((4, 1024), F32)
        ho[0] = jnp.zeros((4, 1024), jnp.int32)
        for h in range(2):
            ua[h, pl.ds(0, 4)] = jnp.zeros((4, 8, 1024), F32)
            uc[h, pl.ds(0, 4)] = jnp.zeros((4, 8, 1024), F32)

    @pl.when(gy == N - 1)
    def _():
        hn[2] = jnp.zeros((4, 1024), F32)
        he[2] = jnp.zeros((4, 1024), F32)
        ho[2] = jnp.zeros((4, 1024), jnp.int32)
        for h in range(2):
            ua[h, pl.ds(8, 4)] = jnp.zeros((4, 8, 1024), F32)
            uc[h, pl.ds(8, 4)] = jnp.zeros((4, 8, 1024), F32)

    hn[1] = north_ref[...]
    he[1] = east_ref[...]
    ho[1] = ocean_ref[...]

    def spread_rows(j, carry):
        for i in range(8):
            v = vert_ref[8 * j + i]
            left = jnp.concatenate([v[0:1], v[0:1], v[2:3], v[2:3]], axis=0)
            right = jnp.concatenate([v[1:2], v[1:2], v[3:4], v[3:4]], axis=0)
            vb[8 * j + i] = jnp.concatenate([left, right], axis=1)
        return carry

    lax.fori_loop(0, 8, spread_rows, 0)

    def factor_row(i, carry):
        v_prev, up_prev = carry
        v = vb[i]
        diagonal = 1.0 + v + v_prev + v_prev * up_prev
        inverse = 1.0 / diagonal
        ratio = v * inverse
        inv_ref[i] = inverse
        fa_ref[i] = v_prev * inverse
        fb_ref[i] = ratio
        return v, -ratio

    zero_row = jnp.zeros((4, 128), F32)
    lax.fori_loop(0, 64, factor_row, (zero_row, zero_row))

    def zero_tile():
        return jnp.zeros((4, 1024), F32)

    def rr_group(i, acc):
        x = res_ref[i // 4, i % 4]
        return acc + x * x

    rr = lax.fori_loop(0, 16, rr_group, zero_tile())

    for group in coef_halos:
        group[1]()

    def coef_row(i, q):
        buf = (hn, he, ho)[q]
        return buf[i // 4, i % 4 : i % 4 + 1, :].astype(F32)

    fn_prev = jnp.zeros((1, 1024), F32)
    for i in range(12):
        m = coef_row(i, 2)
        if i < 11:
            fn = coef_row(i, 0) * m * coef_row(i + 1, 2)
        else:
            fn = jnp.zeros((1, 1024), F32)
        fe = coef_row(i, 1) * m * pltpu.roll(m, 1023, 1)
        fw_e = pltpu.roll(fe, 1, 1)
        centre = m - fn - fn_prev - fe - fw_e
        for q, value in enumerate((centre, fn, fe, fw_e)):
            cf[i, q] = jnp.broadcast_to(value, (8, 1024))
        fn_prev = fn

    def stencil(src, h, i):
        u = src[h, i]
        return (
            cf[i, 0] * u
            + cf[i, 1] * src[h, i + 1]
            + cf[i - 1, 1] * src[h, i - 1]
            + cf[i, 2] * pltpu.roll(u, 1023, 1)
            + cf[i, 3] * pltpu.roll(u, 1, 1)
        )

    def lateral(buf, h):
        src, dst = buf, ub
        for step in range(NSTEP - 1):

            for i in range(1 + step, 11 - step):
                dst[h, i] = stencil(src, h, i)
            src, dst = dst, src
        return src

    low = lax.broadcasted_iota(jnp.int32, (8, 128), 1) < 64

    def swap(a, b):
        return (
            jnp.where(low, a, pltpu.roll(b, 64, 1)),
            jnp.where(low, pltpu.roll(a, 64, 1), b),
        )

    x1 = [
        exchange(
            lambda p, h=h: xs1.at[h, p],
            lambda s, h=h: xr1.at[h, s],
            "gx",
            gx,
            x_send.at[h],
            x_recv.at[h],
        )
        for h in range(2)
    ]
    x2 = [
        exchange(
            lambda p, h=h: xs2.at[h, p],
            lambda s, h=h: xr2.at[h, s],
            "gx",
            gx,
            x_send.at[2 + h],
            x_recv.at[2 + h],
        )
        for h in range(2)
    ]

    for h in range(2):
        first_halo[h][1]()
        src = lateral(ua, h)
        for pair in range(2):
            a = stencil(src, h, 4 + 2 * pair)
            b = stencil(src, h, 5 + 2 * pair)
            for t in range(8):
                lanes = slice(128 * t, 128 * t + 128)
                even, odd = swap(a[:, lanes], b[:, lanes])
                xs1[h, 2 * t, 8 * pair : 8 * pair + 8] = even
                xs1[h, 2 * t + 1, 8 * pair : 8 * pair + 8] = odd
        x1[h][0]()
        xr1[h, gx] = xs1[h, gx]

    def vertical(load, store):
        def forward(j, prev):
            for i in range(8):
                k = 8 * j + i
                prev = load(j, i) * inv_ref[k] + fa_ref[k] * prev
                fw[k] = prev
            return prev

        lax.fori_loop(0, 8, forward, zero_row)

        def backward(k, prev):
            j = 7 - k
            for i in range(7, -1, -1):
                prev = fw[8 * j + i] + fb_ref[8 * j + i] * prev
                store(j, i, prev)
            return prev

        lax.fori_loop(0, 8, backward, zero_row)

    z = gx // 2
    core = gx % 2

    def chip(off):
        return lax.rem(z + off + 8, 8)

    def o1_copy(h, peer, slot):
        return pltpu.make_async_remote_copy(
            src_ref=p_ref.at[h, peer],
            dst_ref=r1.at[h, slot],
            send_sem=o1_send.at[h, peer],
            recv_sem=o1_recv.at[h, slot],
            device_id={"gx": peer},
            device_id_type=pl.DeviceIdType.MESH,
        )

    def o4_copy(h, c, s, k, peer, slot):
        return pltpu.make_async_remote_copy(
            src_ref=u_ref.at[c, s, k, h],
            dst_ref=back.at[h, slot],
            send_sem=o4_send.at[h, peer],
            recv_sem=o4_recv.at[h, slot],
            device_id={"gx": peer},
            device_id_type=pl.DeviceIdType.MESH,
        )

    def peers(c, s, step):
        off = OFFSETS[c][s]
        if off == 0:
            step(1 - core, 2 * z + 1 - core)
        else:
            for k in range(2):
                step(k, 2 * chip(off) + k)

    o2 = [
        exchange(
            lambda p, c=c: t2.at[p // 2, p % 2, c],
            lambda s, c=c: a_ref.at[c, s],
            "gy",
            gy,
            o2_send.at[c],
            o2_recv.at[c],
        )
        for c in range(4)
    ]
    o3 = [
        exchange(
            lambda p, c=c: q_ref.at[c, p],
            lambda s, c=c: b_ref.at[c, s // 2, s % 2],
            "gy",
            gy,
            o3_send.at[c],
            o3_recv.at[c],
        )
        for c in range(4)
    ]

    def columns(h):
        x1[h][1]()

        def load_column(j, i):
            return xr1[h, 2 * j + i // 4, pl.ds(i % 4, 4, stride=4), :]

        def store_column(j, i, value):
            sm[h, pl.ds(8 * j + i, 4, stride=64), :] = value

        vertical(load_column, store_column)
        return split(jnp.concatenate([sm[h, 0:128], sm[h, 128:256]], axis=1))

    def profile(h, c, smoothed):
        for s in range(2):
            j = chip(OFFSETS[c][s])
            rows = pl.ds(pl.multiple_of(128 * j, 128), 128)
            value = dot3(w_hi[rows, :], w_lo[rows, :], *smoothed, ((1,), (1,)))
            p_ref[h, pl.ds(2 * j, 2)] = value.reshape(2, 8, 8, 128)
            peers(c, s, lambda k, peer: o1_copy(h, peer, gx).start())

    smoothed_0 = columns(0)
    profile(0, 0, smoothed_0)
    smoothed_1 = columns(1)
    profile(1, 0, smoothed_1)
    for c in range(1, 4):
        profile(0, c, smoothed_0)
        profile(1, c, smoothed_1)
    for h in range(2):
        r1[h, gx] = p_ref[h, gx]

    top = lax.broadcasted_iota(jnp.int32, (8, 8, 128), 1) < 4

    def mix(a, b):
        return (
            jnp.where(top, a, pltpu.roll(b, 4, 1)),
            jnp.where(top, pltpu.roll(a, 4, 1), b),
        )

    def forward_chunk(c):
        for h in range(2):
            for s in range(2):
                peers(c, s, lambda k, peer: o1_copy(h, peer, peer).wait_recv())
                j = chip(OFFSETS[c][s])
                even, odd = mix(r1[h, 2 * j], r1[h, 2 * j + 1])
                t2[:, 0, c, h, s] = even
                t2[:, 1, c, h, s] = odd
        o2[c][0]()
        a_ref[c, gy] = t2[gy // 2, gy % 2, c]

    def weigh(c):
        o2[c][1]()
        blocks = [a_ref[c, :, h].reshape(256, 128) for h in range(2)]
        hi, lo = split(jnp.concatenate(blocks, axis=1))
        value = dot3(hi, lo, e_hi[...], e_lo[...], ((1,), (0,)))
        for h in range(2):
            q_ref[c, :, h] = value[:, 128 * h : 128 * h + 128].reshape(N, 2, 8, 128)
        o3[c][0]()
        b_ref[c, gy // 2, gy % 2] = q_ref[c, gy]

    def return_chunk(c):
        o3[c][1]()
        for h in range(2):
            for s in range(2):
                even, odd = mix(b_ref[c, :, 0, h, s], b_ref[c, :, 1, h, s])
                u_ref[c, s, 0, h] = even
                u_ref[c, s, 1, h] = odd

    def send_back(c, h):
        for s in range(2):
            peers(c, s, lambda k, peer: o4_copy(h, c, s, k, peer, gx).start())
            if OFFSETS[c][s] == 0:
                back[h, gx] = u_ref[c, s, core, h]

    forward_chunk(0)
    forward_chunk(1)
    weigh(0)
    weigh(1)
    forward_chunk(2)
    return_chunk(0)
    send_back(0, 0)
    send_back(0, 1)
    forward_chunk(3)
    return_chunk(1)
    send_back(1, 0)
    send_back(1, 1)
    weigh(2)
    weigh(3)
    return_chunk(2)
    send_back(2, 0)
    return_chunk(3)
    send_back(3, 0)
    send_back(2, 1)
    send_back(3, 1)

    for h in range(2):
        spread = jnp.zeros((256, 128), F32)
        for c in range(4):
            for s in range(2):
                peers(c, s, lambda k, peer: o4_copy(h, c, s, k, peer, peer).wait_recv())
                j = chip(OFFSETS[c][s])
                cols = pl.ds(pl.multiple_of(128 * j, 128), 128)
                b_hi, b_lo = split(back[h, pl.ds(2 * j, 2)].reshape(128, 128))
                spread = spread + dot3(wt_hi[:, cols], wt_lo[:, cols], b_hi, b_lo, ((1,), (0,)))
        sp[h, 0:128] = spread[0:128].T
        sp[h, 128:256] = spread[128:256].T

        def load_spread(j, i, h=h):
            return sp[h, pl.ds(8 * j + i, 4, stride=64), :]

        def store_spread(j, i, value, h=h):
            xs2[h, 2 * j + i // 4, pl.ds(i % 4, 4, stride=4), :] = value

        vertical(load_spread, store_spread)
        x2[h][0]()
        xr2[h, gx] = xs2[h, gx]

    for h in range(2):
        x2[h][1]()
        for pair in range(2):
            rows = slice(8 * pair, 8 * pair + 8)
            for t in range(8):
                a, b = swap(xr2[h, 2 * t, rows], xr2[h, 2 * t + 1, rows])
                uc[h, 4 + 2 * pair, :, 128 * t : 128 * t + 128] = a
                uc[h, 5 + 2 * pair, :, 128 * t : 128 * t + 128] = b
        second_halo[h][0]()

    sums = (zero_tile(), zero_tile(), zero_tile())
    for h in range(2):
        second_halo[h][1]()
        second_halo[h][2]()
        src = lateral(uc, h)
        for r in range(4):
            tile = stencil(src, h, 4 + r)
            for v in range(2):
                for l in range(4):
                    k = 4 * v + l
                    image_ref[2 * h + v, l, r : r + 1, :] = tile[k : k + 1]

        for i in range(8):
            pq, rq, qq = sums
            v, l = 2 * h + i // 4, i % 4
            d, r = dir_ref[v, l], res_ref[v, l]
            q = d + image_ref[v, l]
            image_ref[v, l] = q
            sums = pq + d * q, rq + r * q, qq + q * q

    def fold(x):
        total = x[:, 0:128]
        for t in range(1, 8):
            total = total + x[:, 128 * t : 128 * t + 128]
        return jnp.sum(total, axis=0, keepdims=True)

    rows = [fold(x) for x in (rr, *sums)]
    part[...] = jnp.concatenate(rows, axis=0)
    g1 = exchange(lambda p: part, lambda s: gat1.at[s], "gx", gx, r_send.at[0], r_recv.at[0])
    g2 = exchange(lambda p: part2, lambda s: gat2.at[s], "gy", gy, r_send.at[1], r_recv.at[1])
    g1[0]()
    gat1[gx] = part[...]
    for group in coef_halos:
        group[2]()
    for h in range(2):
        first_halo[h][2]()
        x1[h][2]()
        for c in range(4):
            for s in range(2):
                peers(c, s, lambda k, peer: o1_copy(h, peer, gx).wait_send())
    g1[1]()
    part2[...] = jnp.sum(gat1[...], axis=0)
    g2[0]()
    gat2[gy] = part2[...]
    for h in range(2):
        x2[h][2]()
        for c in range(4):
            for s in range(2):
                peers(c, s, lambda k, peer: o4_copy(h, c, s, k, peer, gx).wait_send())
    for c in range(4):
        o2[c][2]()
        o3[c][2]()
    g1[2]()
    g2[1]()
    total = jnp.sum(jnp.sum(gat2[...], axis=0), axis=1, keepdims=True)
    norm_now, curvature = total[0:1], total[1:2]
    cross, image_norm = total[2:3], total[3:4]
    alpha = norm_now / curvature
    norm_next = norm_now - 2.0 * alpha * cross + alpha * alpha * image_norm
    beta = norm_next / norm_now
    scal_ref[...] = jnp.concatenate(
        [jnp.broadcast_to(alpha, (4, 128)), jnp.broadcast_to(beta, (4, 128))], axis=0
    )
    g2[2]()


def update(image_ref, scal_ref, dir_ref, sol_ref, res_ref, sol_out, res_out, dir_out):
    alpha = scal_ref[0:1, 0:1]
    beta = scal_ref[4:5, 0:1]

    for v in range(4):
        for l in range(4):
            d = dir_ref[v, l]
            r = res_ref[v, l] - alpha * image_ref[v, l]
            sol_out[v, l] = sol_ref[v, l] + alpha * d
            res_out[v, l] = r
            dir_out[v, l] = r + beta * d


def per_device(
    direction,
    solution,
    residual,
    north_coef,
    east_coef,
    ocean,
    vert_coef,
    obs_owner,
    obs_row,
    obs_col,
    obs_frac,
    error_inverse,
):
    vm = pltpu.VMEM
    dma = pltpu.SemaphoreType.DMA
    field = jax.ShapeDtypeStruct((4, 4, 4, 1024), F32)
    in_vmem = pl.BlockSpec(memory_space=pltpu.VMEM)
    level = vm((64, 4, 128), F32)
    wide = vm((2, 12, 8, 1024), F32)
    swap_buf = vm((2, N, 16, 128), F32)
    image, scal = pl.pallas_call(
        kernel,
        out_shape=(field, jax.ShapeDtypeStruct((8, 128), F32)),
        in_specs=[in_vmem] * 11,
        out_specs=(in_vmem,) * 2,
        scratch_shapes=[
            vm((2, 4, 8, 1024), F32),
            wide,
            wide,
            wide,
            vm((3, 4, 1024), F32),
            vm((3, 4, 1024), F32),
            vm((3, 4, 1024), jnp.int32),
            vm((12, 4, 8, 1024), F32),
            vm((512, 128), F32),
            level,
            level,
            level,
            level,
            level,
            vm((512, 256), BF16),
            vm((512, 256), BF16),
            vm((1024, 256), BF16),
            vm((1024, 256), BF16),
            vm((256, 1024), BF16),
            vm((256, 1024), BF16),
            vm((256, 256), BF16),
            vm((256, 256), BF16),
            swap_buf,
            swap_buf,
            vm((2, 256, 128), F32),
            vm((2, N, 8, 8, 128), F32),
            vm((2, N, 8, 8, 128), F32),
            vm((8, 2, 4, 2, 2, 8, 128), F32),
            vm((4, N, 2, 2, 8, 128), F32),
            vm((4, N, 2, 2, 8, 128), F32),
            vm((4, 8, 2, 2, 2, 8, 128), F32),
            vm((4, 2, 2, 2, 8, 8, 128), F32),
            vm((2, N, 8, 8, 128), F32),
            vm((2, 256, 128), F32),
            swap_buf,
            swap_buf,
            vm((4, 128), F32),
            vm((N, 4, 128), F32),
            vm((4, 128), F32),
            vm((N, 4, 128), F32),
            dma((14,)),
            dma((14,)),
            dma((4, N)),
            dma((4, N)),
            dma((2, N)),
            dma((2, N)),
            dma((4, N)),
            dma((4, N)),
            dma((4, N)),
            dma((4, N)),
            dma((2, N)),
            dma((2, N)),
            dma((2, N)),
            dma((2, N)),
        ],
        compiler_params=pltpu.CompilerParams(collective_id=0, has_side_effects=True),
        name="cg_step",
    )(
        direction,
        residual,
        north_coef,
        east_coef,
        ocean,
        vert_coef,
        obs_owner.reshape(1, 512),
        obs_row.reshape(1, 512),
        obs_col.reshape(1, 512),
        obs_frac.reshape(2, 512),
        error_inverse.reshape(256, 256),
    )
    return pl.pallas_call(
        update,
        out_shape=(field,) * 3,
        in_specs=[in_vmem] * 5,
        out_specs=(in_vmem,) * 3,
        name="cg_update",
    )(image, scal, direction, solution, residual)


def solution(mesh):
    field = P(None, "gx", "gy", None)
    in_specs = (
        field,
        field,
        field,
        P("gy", None),
        P("gy", None),
        P("gy", None),
        P(None, "gy", "gx"),
        P("gy", "gx", None, None),
        P("gy", "gx", None),
        P("gy", "gx", None),
        P("gy", "gx", None, None),
        P("gy", "gx", None, None),
    )
    return jax.shard_map(
        per_device, mesh=mesh, in_specs=in_specs, out_specs=(field,) * 3, check_vma=False
    )
```

```python
import functools

import jax
import jax.numpy as jnp
from jax import lax
from jax.experimental import pallas as pl
from jax.experimental.pallas import tpu as pltpu
from jax.sharding import PartitionSpec as P

NSTEP = 4
N = 16
F32 = jnp.float32
BF16 = jnp.bfloat16


def split(x):
    hi = x.astype(BF16)
    lo = (x - hi.astype(F32)).astype(BF16)
    return hi, lo


def dot(a, b, dims):
    return lax.dot_general(a, b, (dims, ((), ())), preferred_element_type=F32)


def dot3(a_hi, a_lo, b_hi, b_lo, dims):
    return dot(a_hi, b_hi, dims) + (dot(a_hi, b_lo, dims) + dot(a_lo, b_hi, dims))


def far_first(axis, me):
    if axis == "gx":
        z, core = me // 2, me % 2
        chips = [lax.rem(z + off + 8, 8) for off in (4, 3, -3, 2, -2, 1, -1)]
        return [2 * chip + k for chip in chips for k in range(2)] + [2 * z + 1 - core]
    y, x = me // 4, me % 4
    steps = [(dy, dx) for dy in range(4) for dx in range(4) if dy or dx]
    steps.sort(key=lambda d: -(min(d[0], 4 - d[0]) + min(d[1], 4 - d[1])))
    return [lax.rem(y + dy, 4) * 4 + lax.rem(x + dx, 4) for dy, dx in steps]


def exchange(src, dst, axis, me, send_sem, recv_sem):
    def copy(peer, slot):
        return pltpu.make_async_remote_copy(
            src_ref=src(peer),
            dst_ref=dst(slot),
            send_sem=send_sem.at[peer],
            recv_sem=recv_sem.at[slot],
            device_id={axis: peer},
            device_id_type=pl.DeviceIdType.MESH,
        )

    def each(step):
        def body(d, carry):
            step(lax.rem(me + d, N))
            return carry

        lax.fori_loop(1, N, body, 0)

    def start():
        for peer in far_first(axis, me):
            copy(peer, me).start()

    def wait_recv():
        each(lambda peer: copy(peer, peer).wait_recv())

    def wait_send():
        each(lambda peer: copy(peer, peer).wait_send())

    return start, wait_recv, wait_send


OFFSETS = ((0, 4), (2, -2), (3, -3), (1, -1))


def kernel(
    dir_ref,
    north_ref,
    east_ref,
    ocean_ref,
    own_ref,
    row_ref,
    col_ref,
    frac_ref,
    res_any,
    vert_any,
    err_any,
    image_ref,
    scal_ref,
    res_ref,
    vert_ref,
    err_ref,
    dt,
    ua,
    ub,
    uc,
    hn,
    he,
    ho,
    cf,
    obs_ref,
    vb,
    inv_ref,
    fa_ref,
    fb_ref,
    fw,
    c_hi,
    c_lo,
    w_hi,
    w_lo,
    wt_hi,
    wt_lo,
    e_hi,
    e_lo,
    xs1,
    xr1,
    sm,
    p_ref,
    r1,
    t2,
    a_ref,
    q_ref,
    b_ref,
    u_ref,
    back,
    sp,
    xs2,
    xr2,
    part,
    gat1,
    part2,
    gat2,
    hs_send,
    hs_recv,
    x_send,
    x_recv,
    o1_send,
    o1_recv,
    o2_send,
    o2_recv,
    o3_send,
    o3_recv,
    o4_send,
    o4_recv,
    r_send,
    r_recv,
    in_sem,
):
    gy = lax.axis_index("gy")
    gx = lax.axis_index("gx")

    barrier = pltpu.get_barrier_semaphore()

    def greet(d, carry):
        pl.semaphore_signal(
            barrier,
            inc=1,
            device_id={"gx": lax.rem(gx + d, N)},
            device_id_type=pl.DeviceIdType.MESH,
        )
        pl.semaphore_signal(
            barrier,
            inc=1,
            device_id={"gy": lax.rem(gy + d, N)},
            device_id_type=pl.DeviceIdType.MESH,
        )
        return carry

    lax.fori_loop(1, N, greet, 0)

    late = [
        pltpu.make_async_copy(src, dst, in_sem.at[i])
        for i, (src, dst) in enumerate(
            ((vert_any, vert_ref), (err_any, err_ref), (res_any, res_ref))
        )
    ]
    for copy in late:
        copy.start()

    for h in range(2):
        for r in range(4):
            rows = [dir_ref[2 * h + v, l, r : r + 1, :] for v in range(2) for l in range(4)]
            tile = jnp.concatenate(rows, axis=0)
            dt[h, r] = tile
            ua[h, 4 + r] = tile

    owner_row = own_ref[...].astype(F32)
    table = jnp.concatenate(
        [
            owner_row,
            row_ref[...].astype(F32),
            col_ref[...].astype(F32),
            frac_ref[...],
            jnp.zeros((123, 512), F32),
        ],
        axis=0,
    )
    for g in range(4):
        obs_ref[128 * g : 128 * g + 128, :] = table[:, 128 * g : 128 * g + 128].T
    lane512 = lax.broadcasted_iota(jnp.int32, (64, 512), 1)
    sub512 = lax.broadcasted_iota(jnp.int32, (64, 512), 0)
    cell = lax.broadcasted_iota(jnp.int32, (64, 256), 1)
    cell_row = (cell // 64).astype(F32)
    cell_lon = (cell % 64).astype(F32)

    def obs_group(g, rank):
        rows = pl.ds(pl.multiple_of(64 * g, 64), 64)
        block = obs_ref[rows, :]
        o, r, c = block[:, 0:1], block[:, 1:2], block[:, 2:3]
        fr, fc = block[:, 3:4], block[:, 4:5]
        lat = jnp.where(cell_row == r, 1.0 - fr, jnp.where(cell_row == r + 1.0, fr, 0.0))
        lon = jnp.where(cell_lon == c, 1.0 - fc, jnp.where(cell_lon == c + 1.0, fc, 0.0))
        hi, lo = split(lat * lon)
        c_hi[rows, :] = hi
        c_lo[rows, :] = lo
        same = (o == owner_row) & (sub512 + 64 * g < lane512)
        return rank + jnp.sum(jnp.where(same, 1.0, 0.0), axis=0, keepdims=True)

    rank = lax.fori_loop(0, 8, obs_group, jnp.zeros((1, 512), F32))
    owner_int = own_ref[...]
    slot = ((owner_int % N) * N + owner_int // N) * 4 + rank.astype(jnp.int32)

    def slot_group(g, carry):
        base = pl.multiple_of(256 * g, 256)
        sub = lax.broadcasted_iota(jnp.int32, (256, 512), 0) + base
        hot = jnp.where(sub == slot, 1.0, 0.0).astype(BF16)
        rows = pl.ds(base, 256)
        for src, dst, dst_t in ((c_hi, w_hi, wt_hi), (c_lo, w_lo, wt_lo)):
            value = dot(hot, src[...], ((1,), (0,)))
            dst[rows, :] = value.astype(BF16)
            dst_t[:, rows] = value.T.astype(BF16)
        return carry

    lax.fori_loop(0, 4, slot_group, 0)

    pl.semaphore_wait(barrier, 2 * (N - 1))

    def halo_copy(src, dst, sem, toward):
        return pltpu.make_async_remote_copy(
            src_ref=src,
            dst_ref=dst,
            send_sem=hs_send.at[sem],
            recv_sem=hs_recv.at[sem],
            device_id={"gy": toward},
            device_id_type=pl.DeviceIdType.MESH,
        )

    def halo(src, buf, sem):
        def up():
            return halo_copy(src, buf(0), sem, gy + 1)

        def down():
            return halo_copy(src, buf(2), sem + 1, gy - 1)

        def start():
            @pl.when(gy < N - 1)
            def _():
                up().start()

            @pl.when(gy > 0)
            def _():
                down().start()

        def wait_recv():
            @pl.when(gy > 0)
            def _():
                up().wait_recv()

            @pl.when(gy < N - 1)
            def _():
                down().wait_recv()

        def wait_send():
            @pl.when(gy < N - 1)
            def _():
                up().wait_send()

            @pl.when(gy > 0)
            def _():
                down().wait_send()

        return start, wait_recv, wait_send

    coef_halos = [
        halo(north_ref, lambda b: hn.at[b], 0),
        halo(east_ref, lambda b: he.at[b], 2),
        halo(ocean_ref, lambda b: ho.at[b], 4),
    ]
    first_halo = [
        halo(dt.at[h], lambda b, h=h: ua.at[h, pl.ds(4 * b, 4)], 6 + 2 * h) for h in range(2)
    ]
    second_halo = [
        halo(uc.at[h, pl.ds(4, 4)], lambda b, h=h: uc.at[h, pl.ds(4 * b, 4)], 10 + 2 * h)
        for h in range(2)
    ]
    for group in coef_halos:
        group[0]()
    first_halo[0][0]()
    first_halo[1][0]()

    @pl.when(gy == 0)
    def _():
        hn[0] = jnp.zeros((4, 1024), F32)
        he[0] = jnp.zeros((4, 1024), F32)
        ho[0] = jnp.zeros((4, 1024), jnp.int32)
        for h in range(2):
            ua[h, pl.ds(0, 4)] = jnp.zeros((4, 8, 1024), F32)
            uc[h, pl.ds(0, 4)] = jnp.zeros((4, 8, 1024), F32)

    @pl.when(gy == N - 1)
    def _():
        hn[2] = jnp.zeros((4, 1024), F32)
        he[2] = jnp.zeros((4, 1024), F32)
        ho[2] = jnp.zeros((4, 1024), jnp.int32)
        for h in range(2):
            ua[h, pl.ds(8, 4)] = jnp.zeros((4, 8, 1024), F32)
            uc[h, pl.ds(8, 4)] = jnp.zeros((4, 8, 1024), F32)

    hn[1] = north_ref[...]
    he[1] = east_ref[...]
    ho[1] = ocean_ref[...]

    for copy in late:
        copy.wait()
    hi, lo = split(err_ref[...])
    e_hi[...] = hi
    e_lo[...] = lo

    def spread_rows(j, carry):
        for i in range(8):
            v = vert_ref[8 * j + i]
            left = jnp.concatenate([v[0:1], v[0:1], v[2:3], v[2:3]], axis=0)
            right = jnp.concatenate([v[1:2], v[1:2], v[3:4], v[3:4]], axis=0)
            vb[8 * j + i] = jnp.concatenate([left, right], axis=1)
        return carry

    lax.fori_loop(0, 8, spread_rows, 0)

    def factor_row(i, carry):
        v_prev, up_prev = carry
        v = vb[i]
        diagonal = 1.0 + v + v_prev + v_prev * up_prev
        inverse = 1.0 / diagonal
        ratio = v * inverse
        inv_ref[i] = inverse
        fa_ref[i] = v_prev * inverse
        fb_ref[i] = ratio
        return v, -ratio

    zero_row = jnp.zeros((4, 128), F32)
    lax.fori_loop(0, 64, factor_row, (zero_row, zero_row))

    def zero_tile():
        return jnp.zeros((4, 1024), F32)

    def rr_group(i, acc):
        x = res_ref[i // 4, i % 4]
        return acc + x * x

    rr = lax.fori_loop(0, 16, rr_group, zero_tile())

    for group in coef_halos:
        group[1]()

    def coef_row(i, q):
        buf = (hn, he, ho)[q]
        return buf[i // 4, i % 4 : i % 4 + 1, :].astype(F32)

    fn_prev = jnp.zeros((1, 1024), F32)
    for i in range(12):
        m = coef_row(i, 2)
        if i < 11:
            fn = coef_row(i, 0) * m * coef_row(i + 1, 2)
        else:
            fn = jnp.zeros((1, 1024), F32)
        fe = coef_row(i, 1) * m * pltpu.roll(m, 1023, 1)
        fw_e = pltpu.roll(fe, 1, 1)
        centre = m - fn - fn_prev - fe - fw_e
        for q, value in enumerate((centre, fn, fe, fw_e)):
            cf[i, q] = jnp.broadcast_to(value, (8, 1024))
        fn_prev = fn

    def stencil(src, h, i):
        u = src[h, i]
        return (
            cf[i, 0] * u
            + cf[i, 1] * src[h, i + 1]
            + cf[i - 1, 1] * src[h, i - 1]
            + cf[i, 2] * pltpu.roll(u, 1023, 1)
            + cf[i, 3] * pltpu.roll(u, 1, 1)
        )

    def lateral(buf, h):
        src, dst = buf, ub
        for step in range(NSTEP - 1):

            for i in range(1 + step, 11 - step):
                dst[h, i] = stencil(src, h, i)
            src, dst = dst, src
        return src

    low = lax.broadcasted_iota(jnp.int32, (8, 128), 1) < 64

    def swap(a, b):
        return (
            jnp.where(low, a, pltpu.roll(b, 64, 1)),
            jnp.where(low, pltpu.roll(a, 64, 1), b),
        )

    x1 = [
        exchange(
            lambda p, h=h: xs1.at[h, p],
            lambda s, h=h: xr1.at[h, s],
            "gx",
            gx,
            x_send.at[h],
            x_recv.at[h],
        )
        for h in range(2)
    ]
    x2 = [
        exchange(
            lambda p, h=h: xs2.at[h, p],
            lambda s, h=h: xr2.at[h, s],
            "gx",
            gx,
            x_send.at[2 + h],
            x_recv.at[2 + h],
        )
        for h in range(2)
    ]

    for h in range(2):
        first_halo[h][1]()
        src = lateral(ua, h)
        for pair in range(2):
            a = stencil(src, h, 4 + 2 * pair)
            b = stencil(src, h, 5 + 2 * pair)
            for t in range(8):
                lanes = slice(128 * t, 128 * t + 128)
                even, odd = swap(a[:, lanes], b[:, lanes])
                xs1[h, 2 * t, 8 * pair : 8 * pair + 8] = even
                xs1[h, 2 * t + 1, 8 * pair : 8 * pair + 8] = odd
        x1[h][0]()
        xr1[h, gx] = xs1[h, gx]

    def vertical(load, store):
        def forward(j, prev):
            for i in range(8):
                k = 8 * j + i
                prev = load(j, i) * inv_ref[k] + fa_ref[k] * prev
                fw[k] = prev
            return prev

        lax.fori_loop(0, 8, forward, zero_row)

        def backward(k, prev):
            j = 7 - k
            for i in range(7, -1, -1):
                prev = fw[8 * j + i] + fb_ref[8 * j + i] * prev
                store(j, i, prev)
            return prev

        lax.fori_loop(0, 8, backward, zero_row)

    z = gx // 2
    core = gx % 2

    def chip(off):
        return lax.rem(z + off + 8, 8)

    def o1_copy(h, peer, slot):
        return pltpu.make_async_remote_copy(
            src_ref=p_ref.at[h, peer],
            dst_ref=r1.at[h, slot],
            send_sem=o1_send.at[h, peer],
            recv_sem=o1_recv.at[h, slot],
            device_id={"gx": peer},
            device_id_type=pl.DeviceIdType.MESH,
        )

    def o4_copy(h, c, s, k, peer, slot):
        return pltpu.make_async_remote_copy(
            src_ref=u_ref.at[c, s, k, h],
            dst_ref=back.at[h, slot],
            send_sem=o4_send.at[h, peer],
            recv_sem=o4_recv.at[h, slot],
            device_id={"gx": peer},
            device_id_type=pl.DeviceIdType.MESH,
        )

    def peers(c, s, step):
        off = OFFSETS[c][s]
        if off == 0:
            step(1 - core, 2 * z + 1 - core)
        else:
            for k in range(2):
                step(k, 2 * chip(off) + k)

    o2 = [
        exchange(
            lambda p, c=c: t2.at[p // 2, p % 2, c],
            lambda s, c=c: a_ref.at[c, s],
            "gy",
            gy,
            o2_send.at[c],
            o2_recv.at[c],
        )
        for c in range(4)
    ]
    o3 = [
        exchange(
            lambda p, c=c: q_ref.at[c, p],
            lambda s, c=c: b_ref.at[c, s // 2, s % 2],
            "gy",
            gy,
            o3_send.at[c],
            o3_recv.at[c],
        )
        for c in range(4)
    ]

    def columns(h):
        x1[h][1]()

        def load_column(j, i):
            return xr1[h, 2 * j + i // 4, pl.ds(i % 4, 4, stride=4), :]

        def store_column(j, i, value):
            sm[h, pl.ds(8 * j + i, 4, stride=64), :] = value

        vertical(load_column, store_column)
        return split(jnp.concatenate([sm[h, 0:128], sm[h, 128:256]], axis=1))

    def profile(h, c, smoothed):
        for s in range(2):
            j = chip(OFFSETS[c][s])
            rows = pl.ds(pl.multiple_of(128 * j, 128), 128)
            value = dot3(w_hi[rows, :], w_lo[rows, :], *smoothed, ((1,), (1,)))
            p_ref[h, pl.ds(2 * j, 2)] = value.reshape(2, 8, 8, 128)
            peers(c, s, lambda k, peer: o1_copy(h, peer, gx).start())

    smoothed_0 = columns(0)
    profile(0, 0, smoothed_0)
    smoothed_1 = columns(1)
    profile(1, 0, smoothed_1)
    for c in range(1, 4):
        profile(0, c, smoothed_0)
        profile(1, c, smoothed_1)
    for h in range(2):
        r1[h, gx] = p_ref[h, gx]

    top = lax.broadcasted_iota(jnp.int32, (8, 8, 128), 1) < 4

    def mix(a, b):
        return (
            jnp.where(top, a, pltpu.roll(b, 4, 1)),
            jnp.where(top, pltpu.roll(a, 4, 1), b),
        )

    def forward_chunk(c):
        for h in range(2):
            for s in range(2):
                peers(c, s, lambda k, peer: o1_copy(h, peer, peer).wait_recv())
                j = chip(OFFSETS[c][s])
                even, odd = mix(r1[h, 2 * j], r1[h, 2 * j + 1])
                t2[:, 0, c, h, s] = even
                t2[:, 1, c, h, s] = odd
        o2[c][0]()
        a_ref[c, gy] = t2[gy // 2, gy % 2, c]

    def weigh(c):
        o2[c][1]()
        blocks = [a_ref[c, :, h].reshape(256, 128) for h in range(2)]
        hi, lo = split(jnp.concatenate(blocks, axis=1))
        value = dot3(hi, lo, e_hi[...], e_lo[...], ((1,), (0,)))
        for h in range(2):
            q_ref[c, :, h] = value[:, 128 * h : 128 * h + 128].reshape(N, 2, 8, 128)
        o3[c][0]()
        b_ref[c, gy // 2, gy % 2] = q_ref[c, gy]

    def return_chunk(c):
        o3[c][1]()
        for h in range(2):
            for s in range(2):
                even, odd = mix(b_ref[c, :, 0, h, s], b_ref[c, :, 1, h, s])
                u_ref[c, s, 0, h] = even
                u_ref[c, s, 1, h] = odd

    def send_back(c, h):
        for s in range(2):
            peers(c, s, lambda k, peer: o4_copy(h, c, s, k, peer, gx).start())
            if OFFSETS[c][s] == 0:
                back[h, gx] = u_ref[c, s, core, h]

    forward_chunk(0)
    forward_chunk(1)
    weigh(0)
    weigh(1)
    forward_chunk(2)
    return_chunk(0)
    send_back(0, 0)
    send_back(0, 1)
    forward_chunk(3)
    return_chunk(1)
    send_back(1, 0)
    send_back(1, 1)
    weigh(2)
    weigh(3)
    return_chunk(2)
    send_back(2, 0)
    return_chunk(3)
    send_back(3, 0)
    send_back(2, 1)
    send_back(3, 1)

    for h in range(2):
        spread = jnp.zeros((256, 128), F32)
        for c in range(4):
            for s in range(2):
                peers(c, s, lambda k, peer: o4_copy(h, c, s, k, peer, peer).wait_recv())
                j = chip(OFFSETS[c][s])
                cols = pl.ds(pl.multiple_of(128 * j, 128), 128)
                b_hi, b_lo = split(back[h, pl.ds(2 * j, 2)].reshape(128, 128))
                spread = spread + dot3(wt_hi[:, cols], wt_lo[:, cols], b_hi, b_lo, ((1,), (0,)))
        sp[h, 0:128] = spread[0:128].T
        sp[h, 128:256] = spread[128:256].T

        def load_spread(j, i, h=h):
            return sp[h, pl.ds(8 * j + i, 4, stride=64), :]

        def store_spread(j, i, value, h=h):
            xs2[h, 2 * j + i // 4, pl.ds(i % 4, 4, stride=4), :] = value

        vertical(load_spread, store_spread)
        x2[h][0]()
        xr2[h, gx] = xs2[h, gx]

    for h in range(2):
        x2[h][1]()
        for pair in range(2):
            rows = slice(8 * pair, 8 * pair + 8)
            for t in range(8):
                a, b = swap(xr2[h, 2 * t, rows], xr2[h, 2 * t + 1, rows])
                uc[h, 4 + 2 * pair, :, 128 * t : 128 * t + 128] = a
                uc[h, 5 + 2 * pair, :, 128 * t : 128 * t + 128] = b
        second_halo[h][0]()

    sums = (zero_tile(), zero_tile(), zero_tile())
    for h in range(2):
        second_halo[h][1]()
        second_halo[h][2]()
        src = lateral(uc, h)
        for r in range(4):
            tile = stencil(src, h, 4 + r)
            for v in range(2):
                for l in range(4):
                    k = 4 * v + l
                    image_ref[2 * h + v, l, r : r + 1, :] = tile[k : k + 1]

        for i in range(8):
            pq, rq, qq = sums
            v, l = 2 * h + i // 4, i % 4
            d, r = dir_ref[v, l], res_ref[v, l]
            q = d + image_ref[v, l]
            image_ref[v, l] = q
            sums = pq + d * q, rq + r * q, qq + q * q

    def fold(x):
        total = x[:, 0:128]
        for t in range(1, 8):
            total = total + x[:, 128 * t : 128 * t + 128]
        return jnp.sum(total, axis=0, keepdims=True)

    rows = [fold(x) for x in (rr, *sums)]
    part[...] = jnp.concatenate(rows, axis=0)
    g1 = exchange(lambda p: part, lambda s: gat1.at[s], "gx", gx, r_send.at[0], r_recv.at[0])
    g2 = exchange(lambda p: part2, lambda s: gat2.at[s], "gy", gy, r_send.at[1], r_recv.at[1])
    g1[0]()
    gat1[gx] = part[...]
    for group in coef_halos:
        group[2]()
    for h in range(2):
        first_halo[h][2]()
        x1[h][2]()
        for c in range(4):
            for s in range(2):
                peers(c, s, lambda k, peer: o1_copy(h, peer, gx).wait_send())
    g1[1]()
    part2[...] = jnp.sum(gat1[...], axis=0)
    g2[0]()
    gat2[gy] = part2[...]
    for h in range(2):
        x2[h][2]()
        for c in range(4):
            for s in range(2):
                peers(c, s, lambda k, peer: o4_copy(h, c, s, k, peer, gx).wait_send())
    for c in range(4):
        o2[c][2]()
        o3[c][2]()
    g1[2]()
    g2[1]()
    total = jnp.sum(jnp.sum(gat2[...], axis=0), axis=1, keepdims=True)
    norm_now, curvature = total[0:1], total[1:2]
    cross, image_norm = total[2:3], total[3:4]
    alpha = norm_now / curvature
    norm_next = norm_now - 2.0 * alpha * cross + alpha * alpha * image_norm
    beta = norm_next / norm_now
    scal_ref[...] = jnp.concatenate(
        [jnp.broadcast_to(alpha, (4, 128)), jnp.broadcast_to(beta, (4, 128))], axis=0
    )
    g2[2]()


def update(image_ref, scal_ref, dir_ref, sol_ref, res_ref, sol_out, res_out, dir_out):
    alpha = scal_ref[0:1, 0:1]
    beta = scal_ref[4:5, 0:1]

    for v in range(4):
        for l in range(4):
            d = dir_ref[v, l]
            r = res_ref[v, l] - alpha * image_ref[v, l]
            sol_out[v, l] = sol_ref[v, l] + alpha * d
            res_out[v, l] = r
            dir_out[v, l] = r + beta * d


def per_device(
    direction,
    solution,
    residual,
    north_coef,
    east_coef,
    ocean,
    vert_coef,
    obs_owner,
    obs_row,
    obs_col,
    obs_frac,
    error_inverse,
):
    vm = pltpu.VMEM
    dma = pltpu.SemaphoreType.DMA
    field = jax.ShapeDtypeStruct((4, 4, 4, 1024), F32)
    in_vmem = pl.BlockSpec(memory_space=pltpu.VMEM)
    level = vm((64, 4, 128), F32)
    wide = vm((2, 12, 8, 1024), F32)
    swap_buf = vm((2, N, 16, 128), F32)
    image, scal = pl.pallas_call(
        kernel,
        out_shape=(field, jax.ShapeDtypeStruct((8, 128), F32)),
        in_specs=[in_vmem] * 8 + [pl.BlockSpec(memory_space=pl.ANY)] * 3,
        out_specs=(in_vmem,) * 2,
        scratch_shapes=[
            vm((4, 4, 4, 1024), F32),
            vm((64, 4, 64), F32),
            vm((256, 256), F32),
            vm((2, 4, 8, 1024), F32),
            wide,
            wide,
            wide,
            vm((3, 4, 1024), F32),
            vm((3, 4, 1024), F32),
            vm((3, 4, 1024), jnp.int32),
            vm((12, 4, 8, 1024), F32),
            vm((512, 128), F32),
            level,
            level,
            level,
            level,
            level,
            vm((512, 256), BF16),
            vm((512, 256), BF16),
            vm((1024, 256), BF16),
            vm((1024, 256), BF16),
            vm((256, 1024), BF16),
            vm((256, 1024), BF16),
            vm((256, 256), BF16),
            vm((256, 256), BF16),
            swap_buf,
            swap_buf,
            vm((2, 256, 128), F32),
            vm((2, N, 8, 8, 128), F32),
            vm((2, N, 8, 8, 128), F32),
            vm((8, 2, 4, 2, 2, 8, 128), F32),
            vm((4, N, 2, 2, 8, 128), F32),
            vm((4, N, 2, 2, 8, 128), F32),
            vm((4, 8, 2, 2, 2, 8, 128), F32),
            vm((4, 2, 2, 2, 8, 8, 128), F32),
            vm((2, N, 8, 8, 128), F32),
            vm((2, 256, 128), F32),
            swap_buf,
            swap_buf,
            vm((4, 128), F32),
            vm((N, 4, 128), F32),
            vm((4, 128), F32),
            vm((N, 4, 128), F32),
            dma((14,)),
            dma((14,)),
            dma((4, N)),
            dma((4, N)),
            dma((2, N)),
            dma((2, N)),
            dma((4, N)),
            dma((4, N)),
            dma((4, N)),
            dma((4, N)),
            dma((2, N)),
            dma((2, N)),
            dma((2, N)),
            dma((2, N)),
            dma((3,)),
        ],
        compiler_params=pltpu.CompilerParams(collective_id=0, has_side_effects=True),
        name="cg_step",
    )(
        direction,
        north_coef,
        east_coef,
        ocean,
        obs_owner.reshape(1, 512),
        obs_row.reshape(1, 512),
        obs_col.reshape(1, 512),
        obs_frac.reshape(2, 512),
        residual,
        vert_coef,
        error_inverse.reshape(256, 256),
    )
    return pl.pallas_call(
        update,
        out_shape=(field,) * 3,
        in_specs=[in_vmem] * 5,
        out_specs=(in_vmem,) * 3,
        name="cg_update",
    )(image, scal, direction, solution, residual)


def solution(mesh):
    field = P(None, "gx", "gy", None)
    in_specs = (
        field,
        field,
        field,
        P("gy", None),
        P("gy", None),
        P("gy", None),
        P(None, "gy", "gx"),
        P("gy", "gx", None, None),
        P("gy", "gx", None),
        P("gy", "gx", None),
        P("gy", "gx", None, None),
        P("gy", "gx", None, None),
    )
    return jax.shard_map(
        per_device, mesh=mesh, in_specs=in_specs, out_specs=(field,) * 3, check_vma=False
    )
```

```python
import functools

import jax
import jax.numpy as jnp
from jax import lax
from jax.experimental import pallas as pl
from jax.experimental.pallas import tpu as pltpu
from jax.sharding import PartitionSpec as P

NSTEP = 4
N = 16
F32 = jnp.float32
BF16 = jnp.bfloat16


def split(x):
    hi = x.astype(BF16)
    lo = (x - hi.astype(F32)).astype(BF16)
    return hi, lo


def dot(a, b, dims):
    return lax.dot_general(a, b, (dims, ((), ())), preferred_element_type=F32)


def dot3(a_hi, a_lo, b_hi, b_lo, dims):
    return dot(a_hi, b_hi, dims) + (dot(a_hi, b_lo, dims) + dot(a_lo, b_hi, dims))


def far_first(axis, me):
    if axis == "gx":
        z, core = me // 2, me % 2
        chips = [lax.rem(z + off + 8, 8) for off in (4, 3, -3, 2, -2, 1, -1)]
        return [2 * chip + k for chip in chips for k in range(2)] + [2 * z + 1 - core]
    y, x = me // 4, me % 4
    steps = [(dy, dx) for dy in range(4) for dx in range(4) if dy or dx]
    steps.sort(key=lambda d: -(min(d[0], 4 - d[0]) + min(d[1], 4 - d[1])))
    return [lax.rem(y + dy, 4) * 4 + lax.rem(x + dx, 4) for dy, dx in steps]


def exchange(src, dst, axis, me, send_sem, recv_sem):
    def copy(peer, slot):
        return pltpu.make_async_remote_copy(
            src_ref=src(peer),
            dst_ref=dst(slot),
            send_sem=send_sem.at[peer],
            recv_sem=recv_sem.at[slot],
            device_id={axis: peer},
            device_id_type=pl.DeviceIdType.MESH,
        )

    def each(step):
        def body(d, carry):
            step(lax.rem(me + d, N))
            return carry

        lax.fori_loop(1, N, body, 0)

    def start():
        for peer in far_first(axis, me):
            copy(peer, me).start()

    def wait_recv():
        each(lambda peer: copy(peer, peer).wait_recv())

    def wait_send():
        each(lambda peer: copy(peer, peer).wait_send())

    return start, wait_recv, wait_send


OFFSETS = ((0, 4), (2, -2), (3, -3), (1, -1))


def kernel(
    dir_ref,
    north_ref,
    east_ref,
    ocean_ref,
    own_ref,
    row_ref,
    col_ref,
    frac_ref,
    res_any,
    vert_any,
    err_any,
    image_ref,
    scal_ref,
    res_ref,
    vert_ref,
    err_ref,
    dt,
    ua,
    ub,
    uc,
    hn,
    he,
    ho,
    cf,
    obs_ref,
    vb,
    inv_ref,
    fa_ref,
    fb_ref,
    fw,
    c_hi,
    c_lo,
    w_hi,
    w_lo,
    wt_hi,
    wt_lo,
    e_hi,
    e_lo,
    xs1,
    xr1,
    sm,
    p_ref,
    r1,
    t2,
    a_ref,
    q_ref,
    b_ref,
    u_ref,
    back,
    sp,
    xs2,
    xr2,
    part,
    gat1,
    part2,
    gat2,
    hs_send,
    hs_recv,
    x_send,
    x_recv,
    o1_send,
    o1_recv,
    o2_send,
    o2_recv,
    o3_send,
    o3_recv,
    o4_send,
    o4_recv,
    r_send,
    r_recv,
    in_sem,
):
    gy = lax.axis_index("gy")
    gx = lax.axis_index("gx")

    barrier = pltpu.get_barrier_semaphore()

    for axis, me in (("gx", gx), ("gy", gy)):
        for peer in far_first(axis, me):
            pl.semaphore_signal(
                barrier, inc=1, device_id={axis: peer}, device_id_type=pl.DeviceIdType.MESH
            )

    late = [
        pltpu.make_async_copy(src, dst, in_sem.at[i])
        for i, (src, dst) in enumerate(
            ((vert_any, vert_ref), (err_any, err_ref), (res_any, res_ref))
        )
    ]
    for copy in late:
        copy.start()

    for h in range(2):
        for r in range(4):
            rows = [dir_ref[2 * h + v, l, r : r + 1, :] for v in range(2) for l in range(4)]
            tile = jnp.concatenate(rows, axis=0)
            dt[h, r] = tile
            ua[h, 4 + r] = tile

    owner_row = own_ref[...].astype(F32)
    table = jnp.concatenate(
        [
            owner_row,
            row_ref[...].astype(F32),
            col_ref[...].astype(F32),
            frac_ref[...],
            jnp.zeros((123, 512), F32),
        ],
        axis=0,
    )
    for g in range(4):
        obs_ref[128 * g : 128 * g + 128, :] = table[:, 128 * g : 128 * g + 128].T
    lane512 = lax.broadcasted_iota(jnp.int32, (64, 512), 1)
    sub512 = lax.broadcasted_iota(jnp.int32, (64, 512), 0)
    cell = lax.broadcasted_iota(jnp.int32, (64, 256), 1)
    cell_row = (cell // 64).astype(F32)
    cell_lon = (cell % 64).astype(F32)

    def obs_group(g, rank):
        rows = pl.ds(pl.multiple_of(64 * g, 64), 64)
        block = obs_ref[rows, :]
        o, r, c = block[:, 0:1], block[:, 1:2], block[:, 2:3]
        fr, fc = block[:, 3:4], block[:, 4:5]
        lat = jnp.where(cell_row == r, 1.0 - fr, jnp.where(cell_row == r + 1.0, fr, 0.0))
        lon = jnp.where(cell_lon == c, 1.0 - fc, jnp.where(cell_lon == c + 1.0, fc, 0.0))
        hi, lo = split(lat * lon)
        c_hi[rows, :] = hi
        c_lo[rows, :] = lo
        same = (o == owner_row) & (sub512 + 64 * g < lane512)
        return rank + jnp.sum(jnp.where(same, 1.0, 0.0), axis=0, keepdims=True)

    rank = lax.fori_loop(0, 8, obs_group, jnp.zeros((1, 512), F32))
    owner_int = own_ref[...]
    slot = ((owner_int % N) * N + owner_int // N) * 4 + rank.astype(jnp.int32)

    def slot_group(g, carry):
        base = pl.multiple_of(256 * g, 256)
        sub = lax.broadcasted_iota(jnp.int32, (256, 512), 0) + base
        hot = jnp.where(sub == slot, 1.0, 0.0).astype(BF16)
        rows = pl.ds(base, 256)
        for src, dst, dst_t in ((c_hi, w_hi, wt_hi), (c_lo, w_lo, wt_lo)):
            value = dot(hot, src[...], ((1,), (0,)))
            dst[rows, :] = value.astype(BF16)
            dst_t[:, rows] = value.T.astype(BF16)
        return carry

    lax.fori_loop(0, 4, slot_group, 0)

    pl.semaphore_wait(barrier, 2 * (N - 1))

    def halo_copy(src, dst, sem, toward):
        return pltpu.make_async_remote_copy(
            src_ref=src,
            dst_ref=dst,
            send_sem=hs_send.at[sem],
            recv_sem=hs_recv.at[sem],
            device_id={"gy": toward},
            device_id_type=pl.DeviceIdType.MESH,
        )

    def halo(src, buf, sem):
        def up():
            return halo_copy(src, buf(0), sem, gy + 1)

        def down():
            return halo_copy(src, buf(2), sem + 1, gy - 1)

        def start():
            @pl.when(gy < N - 1)
            def _():
                up().start()

            @pl.when(gy > 0)
            def _():
                down().start()

        def wait_recv():
            @pl.when(gy > 0)
            def _():
                up().wait_recv()

            @pl.when(gy < N - 1)
            def _():
                down().wait_recv()

        def wait_send():
            @pl.when(gy < N - 1)
            def _():
                up().wait_send()

            @pl.when(gy > 0)
            def _():
                down().wait_send()

        return start, wait_recv, wait_send

    coef_halos = [
        halo(north_ref, lambda b: hn.at[b], 0),
        halo(east_ref, lambda b: he.at[b], 2),
        halo(ocean_ref, lambda b: ho.at[b], 4),
    ]
    first_halo = [
        halo(dt.at[h], lambda b, h=h: ua.at[h, pl.ds(4 * b, 4)], 6 + 2 * h) for h in range(2)
    ]
    second_halo = [
        halo(uc.at[h, pl.ds(4, 4)], lambda b, h=h: uc.at[h, pl.ds(4 * b, 4)], 10 + 2 * h)
        for h in range(2)
    ]
    for group in coef_halos:
        group[0]()
    first_halo[0][0]()
    first_halo[1][0]()

    @pl.when(gy == 0)
    def _():
        hn[0] = jnp.zeros((4, 1024), F32)
        he[0] = jnp.zeros((4, 1024), F32)
        ho[0] = jnp.zeros((4, 1024), jnp.int32)
        for h in range(2):
            ua[h, pl.ds(0, 4)] = jnp.zeros((4, 8, 1024), F32)
            uc[h, pl.ds(0, 4)] = jnp.zeros((4, 8, 1024), F32)

    @pl.when(gy == N - 1)
    def _():
        hn[2] = jnp.zeros((4, 1024), F32)
        he[2] = jnp.zeros((4, 1024), F32)
        ho[2] = jnp.zeros((4, 1024), jnp.int32)
        for h in range(2):
            ua[h, pl.ds(8, 4)] = jnp.zeros((4, 8, 1024), F32)
            uc[h, pl.ds(8, 4)] = jnp.zeros((4, 8, 1024), F32)

    hn[1] = north_ref[...]
    he[1] = east_ref[...]
    ho[1] = ocean_ref[...]

    for copy in late:
        copy.wait()
    hi, lo = split(err_ref[...])
    e_hi[...] = hi
    e_lo[...] = lo

    def spread_rows(j, carry):
        for i in range(8):
            v = vert_ref[8 * j + i]
            left = jnp.concatenate([v[0:1], v[0:1], v[2:3], v[2:3]], axis=0)
            right = jnp.concatenate([v[1:2], v[1:2], v[3:4], v[3:4]], axis=0)
            vb[8 * j + i] = jnp.concatenate([left, right], axis=1)
        return carry

    lax.fori_loop(0, 8, spread_rows, 0)

    def factor_row(i, carry):
        v_prev, up_prev = carry
        v = vb[i]
        diagonal = 1.0 + v + v_prev + v_prev * up_prev
        inverse = 1.0 / diagonal
        ratio = v * inverse
        inv_ref[i] = inverse
        fa_ref[i] = v_prev * inverse
        fb_ref[i] = ratio
        return v, -ratio

    zero_row = jnp.zeros((4, 128), F32)
    lax.fori_loop(0, 64, factor_row, (zero_row, zero_row))

    def zero_tile():
        return jnp.zeros((4, 1024), F32)

    def rr_group(i, acc):
        x = res_ref[i // 4, i % 4]
        return acc + x * x

    rr = lax.fori_loop(0, 16, rr_group, zero_tile())

    for group in coef_halos:
        group[1]()

    def coef_row(i, q):
        buf = (hn, he, ho)[q]
        return buf[i // 4, i % 4 : i % 4 + 1, :].astype(F32)

    fn_prev = jnp.zeros((1, 1024), F32)
    for i in range(12):
        m = coef_row(i, 2)
        if i < 11:
            fn = coef_row(i, 0) * m * coef_row(i + 1, 2)
        else:
            fn = jnp.zeros((1, 1024), F32)
        fe = coef_row(i, 1) * m * pltpu.roll(m, 1023, 1)
        fw_e = pltpu.roll(fe, 1, 1)
        centre = m - fn - fn_prev - fe - fw_e
        for q, value in enumerate((centre, fn, fe, fw_e)):
            cf[i, q] = jnp.broadcast_to(value, (8, 1024))
        fn_prev = fn

    def stencil(src, h, i):
        u = src[h, i]
        return (
            cf[i, 0] * u
            + cf[i, 1] * src[h, i + 1]
            + cf[i - 1, 1] * src[h, i - 1]
            + cf[i, 2] * pltpu.roll(u, 1023, 1)
            + cf[i, 3] * pltpu.roll(u, 1, 1)
        )

    def lateral(buf, h):
        src, dst = buf, ub
        for step in range(NSTEP - 1):

            for i in range(1 + step, 11 - step):
                dst[h, i] = stencil(src, h, i)
            src, dst = dst, src
        return src

    low = lax.broadcasted_iota(jnp.int32, (8, 128), 1) < 64

    def swap(a, b):
        return (
            jnp.where(low, a, pltpu.roll(b, 64, 1)),
            jnp.where(low, pltpu.roll(a, 64, 1), b),
        )

    x1 = [
        exchange(
            lambda p, h=h: xs1.at[h, p],
            lambda s, h=h: xr1.at[h, s],
            "gx",
            gx,
            x_send.at[h],
            x_recv.at[h],
        )
        for h in range(2)
    ]
    x2 = [
        exchange(
            lambda p, h=h: xs2.at[h, p],
            lambda s, h=h: xr2.at[h, s],
            "gx",
            gx,
            x_send.at[2 + h],
            x_recv.at[2 + h],
        )
        for h in range(2)
    ]

    for h in range(2):
        first_halo[h][1]()
        src = lateral(ua, h)
        for pair in range(2):
            a = stencil(src, h, 4 + 2 * pair)
            b = stencil(src, h, 5 + 2 * pair)
            for t in range(8):
                lanes = slice(128 * t, 128 * t + 128)
                even, odd = swap(a[:, lanes], b[:, lanes])
                xs1[h, 2 * t, 8 * pair : 8 * pair + 8] = even
                xs1[h, 2 * t + 1, 8 * pair : 8 * pair + 8] = odd
        x1[h][0]()
        xr1[h, gx] = xs1[h, gx]

    def vertical(load, store):
        def forward(j, prev):
            for i in range(8):
                k = 8 * j + i
                prev = load(j, i) * inv_ref[k] + fa_ref[k] * prev
                fw[k] = prev
            return prev

        lax.fori_loop(0, 8, forward, zero_row)

        def backward(k, prev):
            j = 7 - k
            for i in range(7, -1, -1):
                prev = fw[8 * j + i] + fb_ref[8 * j + i] * prev
                store(j, i, prev)
            return prev

        lax.fori_loop(0, 8, backward, zero_row)

    z = gx // 2
    core = gx % 2

    def chip(off):
        return lax.rem(z + off + 8, 8)

    def o1_copy(h, peer, slot):
        return pltpu.make_async_remote_copy(
            src_ref=p_ref.at[h, peer],
            dst_ref=r1.at[h, slot],
            send_sem=o1_send.at[h, peer],
            recv_sem=o1_recv.at[h, slot],
            device_id={"gx": peer},
            device_id_type=pl.DeviceIdType.MESH,
        )

    def o4_copy(h, c, s, k, peer, slot):
        return pltpu.make_async_remote_copy(
            src_ref=u_ref.at[c, s, k, h],
            dst_ref=back.at[h, slot],
            send_sem=o4_send.at[h, peer],
            recv_sem=o4_recv.at[h, slot],
            device_id={"gx": peer},
            device_id_type=pl.DeviceIdType.MESH,
        )

    def peers(c, s, step):
        off = OFFSETS[c][s]
        if off == 0:
            step(1 - core, 2 * z + 1 - core)
        else:
            for k in range(2):
                step(k, 2 * chip(off) + k)

    o2 = [
        exchange(
            lambda p, c=c: t2.at[p // 2, p % 2, c],
            lambda s, c=c: a_ref.at[c, s],
            "gy",
            gy,
            o2_send.at[c],
            o2_recv.at[c],
        )
        for c in range(4)
    ]
    o3 = [
        exchange(
            lambda p, c=c: q_ref.at[c, p],
            lambda s, c=c: b_ref.at[c, s // 2, s % 2],
            "gy",
            gy,
            o3_send.at[c],
            o3_recv.at[c],
        )
        for c in range(4)
    ]

    def columns(h):
        x1[h][1]()

        def load_column(j, i):
            return xr1[h, 2 * j + i // 4, pl.ds(i % 4, 4, stride=4), :]

        def store_column(j, i, value):
            sm[h, pl.ds(8 * j + i, 4, stride=64), :] = value

        vertical(load_column, store_column)
        return split(jnp.concatenate([sm[h, 0:128], sm[h, 128:256]], axis=1))

    def profile(h, c, smoothed):
        for s in range(2):
            j = chip(OFFSETS[c][s])
            rows = pl.ds(pl.multiple_of(128 * j, 128), 128)
            value = dot3(w_hi[rows, :], w_lo[rows, :], *smoothed, ((1,), (1,)))
            p_ref[h, pl.ds(2 * j, 2)] = value.reshape(2, 8, 8, 128)
            peers(c, s, lambda k, peer: o1_copy(h, peer, gx).start())

    smoothed_0 = columns(0)
    profile(0, 0, smoothed_0)
    profile(0, 1, smoothed_0)
    smoothed_1 = columns(1)
    profile(1, 0, smoothed_1)
    profile(1, 1, smoothed_1)
    for c in range(2, 4):
        profile(0, c, smoothed_0)
        profile(1, c, smoothed_1)
    for h in range(2):
        r1[h, gx] = p_ref[h, gx]

    top = lax.broadcasted_iota(jnp.int32, (8, 8, 128), 1) < 4

    def mix(a, b):
        return (
            jnp.where(top, a, pltpu.roll(b, 4, 1)),
            jnp.where(top, pltpu.roll(a, 4, 1), b),
        )

    def forward_chunk(c):
        for h in range(2):
            for s in range(2):
                peers(c, s, lambda k, peer: o1_copy(h, peer, peer).wait_recv())
                j = chip(OFFSETS[c][s])
                even, odd = mix(r1[h, 2 * j], r1[h, 2 * j + 1])
                t2[:, 0, c, h, s] = even
                t2[:, 1, c, h, s] = odd
        o2[c][0]()
        a_ref[c, gy] = t2[gy // 2, gy % 2, c]

    def weigh(c):
        o2[c][1]()
        blocks = [a_ref[c, :, h].reshape(256, 128) for h in range(2)]
        hi, lo = split(jnp.concatenate(blocks, axis=1))
        value = dot3(hi, lo, e_hi[...], e_lo[...], ((1,), (0,)))
        for h in range(2):
            q_ref[c, :, h] = value[:, 128 * h : 128 * h + 128].reshape(N, 2, 8, 128)
        o3[c][0]()
        b_ref[c, gy // 2, gy % 2] = q_ref[c, gy]

    def return_chunk(c):
        o3[c][1]()
        for h in range(2):
            for s in range(2):
                even, odd = mix(b_ref[c, :, 0, h, s], b_ref[c, :, 1, h, s])
                u_ref[c, s, 0, h] = even
                u_ref[c, s, 1, h] = odd

    def send_back(c, h):
        for s in range(2):
            peers(c, s, lambda k, peer: o4_copy(h, c, s, k, peer, gx).start())
            if OFFSETS[c][s] == 0:
                back[h, gx] = u_ref[c, s, core, h]

    forward_chunk(0)
    forward_chunk(1)
    weigh(0)
    weigh(1)
    forward_chunk(2)
    return_chunk(0)
    send_back(0, 0)
    send_back(0, 1)
    forward_chunk(3)
    return_chunk(1)
    send_back(1, 0)
    send_back(1, 1)
    weigh(2)
    weigh(3)
    return_chunk(2)
    send_back(2, 0)
    return_chunk(3)
    send_back(3, 0)
    send_back(2, 1)
    send_back(3, 1)

    for h in range(2):
        spread = jnp.zeros((256, 128), F32)
        for c in range(4):
            for s in range(2):
                peers(c, s, lambda k, peer: o4_copy(h, c, s, k, peer, peer).wait_recv())
                j = chip(OFFSETS[c][s])
                cols = pl.ds(pl.multiple_of(128 * j, 128), 128)
                b_hi, b_lo = split(back[h, pl.ds(2 * j, 2)].reshape(128, 128))
                spread = spread + dot3(wt_hi[:, cols], wt_lo[:, cols], b_hi, b_lo, ((1,), (0,)))
        sp[h, 0:128] = spread[0:128].T
        sp[h, 128:256] = spread[128:256].T

        def load_spread(j, i, h=h):
            return sp[h, pl.ds(8 * j + i, 4, stride=64), :]

        def store_spread(j, i, value, h=h):
            xs2[h, 2 * j + i // 4, pl.ds(i % 4, 4, stride=4), :] = value

        vertical(load_spread, store_spread)
        x2[h][0]()
        xr2[h, gx] = xs2[h, gx]

    for h in range(2):
        x2[h][1]()
        for pair in range(2):
            rows = slice(8 * pair, 8 * pair + 8)
            for t in range(8):
                a, b = swap(xr2[h, 2 * t, rows], xr2[h, 2 * t + 1, rows])
                uc[h, 4 + 2 * pair, :, 128 * t : 128 * t + 128] = a
                uc[h, 5 + 2 * pair, :, 128 * t : 128 * t + 128] = b
        second_halo[h][0]()

    sums = (zero_tile(), zero_tile(), zero_tile())
    for h in range(2):
        second_halo[h][1]()
        second_halo[h][2]()
        src = lateral(uc, h)
        for r in range(4):
            tile = stencil(src, h, 4 + r)
            for v in range(2):
                for l in range(4):
                    k = 4 * v + l
                    image_ref[2 * h + v, l, r : r + 1, :] = tile[k : k + 1]

        for i in range(8):
            pq, rq, qq = sums
            v, l = 2 * h + i // 4, i % 4
            d, r = dir_ref[v, l], res_ref[v, l]
            q = d + image_ref[v, l]
            image_ref[v, l] = q
            sums = pq + d * q, rq + r * q, qq + q * q

    def fold(x):
        total = x[:, 0:128]
        for t in range(1, 8):
            total = total + x[:, 128 * t : 128 * t + 128]
        return jnp.sum(total, axis=0, keepdims=True)

    rows = [fold(x) for x in (rr, *sums)]
    part[...] = jnp.concatenate(rows, axis=0)
    g1 = exchange(lambda p: part, lambda s: gat1.at[s], "gx", gx, r_send.at[0], r_recv.at[0])
    g2 = exchange(lambda p: part2, lambda s: gat2.at[s], "gy", gy, r_send.at[1], r_recv.at[1])
    g1[0]()
    gat1[gx] = part[...]
    for group in coef_halos:
        group[2]()
    for h in range(2):
        first_halo[h][2]()
        x1[h][2]()
        for c in range(4):
            for s in range(2):
                peers(c, s, lambda k, peer: o1_copy(h, peer, gx).wait_send())
    g1[1]()
    part2[...] = jnp.sum(gat1[...], axis=0)
    g2[0]()
    gat2[gy] = part2[...]
    for h in range(2):
        x2[h][2]()
        for c in range(4):
            for s in range(2):
                peers(c, s, lambda k, peer: o4_copy(h, c, s, k, peer, gx).wait_send())
    for c in range(4):
        o2[c][2]()
        o3[c][2]()
    g1[2]()
    g2[1]()
    total = jnp.sum(jnp.sum(gat2[...], axis=0), axis=1, keepdims=True)
    norm_now, curvature = total[0:1], total[1:2]
    cross, image_norm = total[2:3], total[3:4]
    alpha = norm_now / curvature
    norm_next = norm_now - 2.0 * alpha * cross + alpha * alpha * image_norm
    beta = norm_next / norm_now
    scal_ref[...] = jnp.concatenate(
        [jnp.broadcast_to(alpha, (4, 128)), jnp.broadcast_to(beta, (4, 128))], axis=0
    )
    g2[2]()


def update(image_ref, scal_ref, dir_ref, sol_ref, res_ref, sol_out, res_out, dir_out):
    alpha = scal_ref[0:1, 0:1]
    beta = scal_ref[4:5, 0:1]

    for v in range(4):
        for l in range(4):
            d = dir_ref[v, l]
            r = res_ref[v, l] - alpha * image_ref[v, l]
            sol_out[v, l] = sol_ref[v, l] + alpha * d
            res_out[v, l] = r
            dir_out[v, l] = r + beta * d


def per_device(
    direction,
    solution,
    residual,
    north_coef,
    east_coef,
    ocean,
    vert_coef,
    obs_owner,
    obs_row,
    obs_col,
    obs_frac,
    error_inverse,
):
    vm = pltpu.VMEM
    dma = pltpu.SemaphoreType.DMA
    field = jax.ShapeDtypeStruct((4, 4, 4, 1024), F32)
    in_vmem = pl.BlockSpec(memory_space=pltpu.VMEM)
    level = vm((64, 4, 128), F32)
    wide = vm((2, 12, 8, 1024), F32)
    swap_buf = vm((2, N, 16, 128), F32)
    image, scal = pl.pallas_call(
        kernel,
        out_shape=(field, jax.ShapeDtypeStruct((8, 128), F32)),
        in_specs=[in_vmem] * 8 + [pl.BlockSpec(memory_space=pl.ANY)] * 3,
        out_specs=(in_vmem,) * 2,
        scratch_shapes=[
            vm((4, 4, 4, 1024), F32),
            vm((64, 4, 64), F32),
            vm((256, 256), F32),
            vm((2, 4, 8, 1024), F32),
            wide,
            wide,
            wide,
            vm((3, 4, 1024), F32),
            vm((3, 4, 1024), F32),
            vm((3, 4, 1024), jnp.int32),
            vm((12, 4, 8, 1024), F32),
            vm((512, 128), F32),
            level,
            level,
            level,
            level,
            level,
            vm((512, 256), BF16),
            vm((512, 256), BF16),
            vm((1024, 256), BF16),
            vm((1024, 256), BF16),
            vm((256, 1024), BF16),
            vm((256, 1024), BF16),
            vm((256, 256), BF16),
            vm((256, 256), BF16),
            swap_buf,
            swap_buf,
            vm((2, 256, 128), F32),
            vm((2, N, 8, 8, 128), F32),
            vm((2, N, 8, 8, 128), F32),
            vm((8, 2, 4, 2, 2, 8, 128), F32),
            vm((4, N, 2, 2, 8, 128), F32),
            vm((4, N, 2, 2, 8, 128), F32),
            vm((4, 8, 2, 2, 2, 8, 128), F32),
            vm((4, 2, 2, 2, 8, 8, 128), F32),
            vm((2, N, 8, 8, 128), F32),
            vm((2, 256, 128), F32),
            swap_buf,
            swap_buf,
            vm((4, 128), F32),
            vm((N, 4, 128), F32),
            vm((4, 128), F32),
            vm((N, 4, 128), F32),
            dma((14,)),
            dma((14,)),
            dma((4, N)),
            dma((4, N)),
            dma((2, N)),
            dma((2, N)),
            dma((4, N)),
            dma((4, N)),
            dma((4, N)),
            dma((4, N)),
            dma((2, N)),
            dma((2, N)),
            dma((2, N)),
            dma((2, N)),
            dma((3,)),
        ],
        compiler_params=pltpu.CompilerParams(collective_id=0, has_side_effects=True),
        name="cg_step",
    )(
        direction,
        north_coef,
        east_coef,
        ocean,
        obs_owner.reshape(1, 512),
        obs_row.reshape(1, 512),
        obs_col.reshape(1, 512),
        obs_frac.reshape(2, 512),
        residual,
        vert_coef,
        error_inverse.reshape(256, 256),
    )
    return pl.pallas_call(
        update,
        out_shape=(field,) * 3,
        in_specs=[in_vmem] * 5,
        out_specs=(in_vmem,) * 3,
        name="cg_update",
    )(image, scal, direction, solution, residual)


def solution(mesh):
    field = P(None, "gx", "gy", None)
    in_specs = (
        field,
        field,
        field,
        P("gy", None),
        P("gy", None),
        P("gy", None),
        P(None, "gy", "gx"),
        P("gy", "gx", None, None),
        P("gy", "gx", None),
        P("gy", "gx", None),
        P("gy", "gx", None, None),
        P("gy", "gx", None, None),
    )
    return jax.shard_map(
        per_device, mesh=mesh, in_specs=in_specs, out_specs=(field,) * 3, check_vma=False
    )
```
